32 devices in a mesh: tile: 8 (over z, y), depth: 4 (over x, core).
Axes of the slice: x: 2, y: 2, z: 4, core: 2. Of those that a mesh axis runs over, the one named last changes fastest.
Arguments:
- owned_blocks: bfloat16 [4, 512, 32768], P('depth', 'tile'), may hold values from -6 to 6
- slot_counts: int32 [4, 8], P('depth'), may hold values from 1 to 64, 256 in all within a row
- brick_order: int32 [4, 8], P('depth'), may hold values from 0 to 7, each once within a row
- view_flip: int32 [8], replicated, may hold values from 0 to 1
- tf_centers: float32 [8], replicated, may hold values from -2.5 to 2.5
- tf_amps: float32 [4, 8], replicated, may hold values from -6 to 6
Outputs:
- image: float32 [4, 128, 1024], P(None, 'depth', 'tile')
The draws below stay inside these ranges and needn't reach their ends.
Inputs may be any that keep to these rules, and one draw needn't show every extreme that they name: `slot_counts`: every row sums to 256, and some entry of every row equals 64. `brick_order`: every row holds each of 0 to 7 once.
All inputs are finite; a program needn't handle non-finite values.
Results may differ from the reference program's by a relative error of at most 0.0003.
Values may be sent and summed in bfloat16 or wider, within the bound.
No kernel may reach another device: no remote copies, remote signals or barrier semaphores. Data moves between devices by JAX's collectives and lax.ppermute only.
A program may use at most 64 MiB of HBM per device.

```python
import math
import jax
import jax.numpy as jnp
import numpy as np

BLOCK = 32
BX = 4
BY = 4
DB = 2
KNOTS = 8
BRICK_BLOCKS = 32
SLOTS = 64
CELLS = 32768
NX = 1024
NY = 128
NZ = 256
N_TILE = 8
N_DEPTH = 4


def touch_ends(values, stream_key, smallest, largest):
    extent = values.shape
    index_at = [jax.random.randint(jax.random.fold_in(stream_key, axis), (), 0, extent[axis]) for axis in range(len(extent))]
    values = values.at[tuple(index_at)].set(smallest)
    longest = extent.index(max(extent))
    index_at[longest] = (index_at[longest] + 1) % extent[longest]
    return values.at[tuple(index_at)].set(largest)


def block_scale(own_key, dims, shards, low, top_value):
    def one(dim, parts):
        steps = jax.random.uniform(jax.random.fold_in(jax.random.fold_in(own_key, 6), dim), (parts,), jnp.float32, low / len(shards), top_value / len(shards))
        return jnp.repeat(jnp.exp(steps), dims[dim] // parts).reshape((-1,) + (1,) * (len(dims) - dim - 1))

    loudness = one(*shards[0])
    for cut in shards[1:]:
        loudness = loudness * one(*cut)
    return loudness


def profile(number_of, total, reach, slope):
    loads = [(1 << 20) // math.isqrt(grade ** slope) + 1 for grade in range(2, number_of + 1)]
    rest, given = total - reach - (number_of - 1), [1] * (number_of - 1)
    while rest > 0:
        movable = [i for i in range(number_of - 1) if given[i] < reach]
        mass, remaining = sum([loads[i] for i in movable]), rest
        for i in movable:
            addition = min(reach - given[i], max(1, remaining * loads[i] // mass), rest)
            given[i] = given[i] + addition
            rest = rest - addition
    return np.array([reach] + given)


def ragged(key, number_of, total, most, slope):
    if number_of == 2:
        one = jax.random.randint(key, (), max(1, total - most), min(most, total - 1) + 1)
        return jnp.stack([one, total - one])
    tallies = jnp.asarray(profile(number_of, total, most, slope), jnp.int32)
    couples = (number_of - 1) // 2
    giver, receiver = tallies[1:1 + 2 * couples:2], tallies[2:2 + 2 * couples:2]
    margin = jnp.minimum(giver - 1, most - receiver)
    moved = jax.random.randint(jax.random.fold_in(key, 1), (couples,), 0, 1 << 20) % (margin + 1)
    tallies = tallies.at[1:1 + 2 * couples:2].set(giver - moved).at[2:2 + 2 * couples:2].set(receiver + moved)
    return tallies[jax.random.permutation(jax.random.fold_in(key, 2), number_of)]


def gaussian(key, dims, deviation, most, pieces=(), kind=jnp.bfloat16):
    drawn = jax.random.normal(key, dims, jnp.float32) * deviation
    if len(pieces) > 0:
        drawn = block_scale(key, dims, pieces, -0.22, 0.18) * drawn
    return jnp.clip(drawn, min=-most, max=most).astype(kind)


def setup_inputs(seed: int = 0) -> dict:
    streams_of = jax.random.split(jax.random.key(seed), 7)
    return {
        "owned_blocks": gaussian(streams_of[0], (N_DEPTH, N_TILE * SLOTS, CELLS), 1.0, 6.0, ((0, 4), (1, 8))),
        "slot_counts": jax.vmap(lambda own: ragged(own, N_TILE, N_TILE * BRICK_BLOCKS, SLOTS, 2))(jax.random.split(streams_of[1], N_DEPTH)).reshape((N_DEPTH, N_TILE)).astype(jnp.int32),
        "brick_order": jax.vmap(lambda own: jax.random.permutation(own, N_TILE))(jax.random.split(streams_of[2], N_DEPTH)).reshape((N_DEPTH, N_TILE)).astype(jnp.int32),
        "view_flip": touch_ends(jax.random.randint(streams_of[3], (N_TILE,), 0, 2), jax.random.fold_in(streams_of[3], 1), 0, 1).astype(jnp.int32),
        "tf_centers": jnp.clip(jax.random.uniform(streams_of[4], (KNOTS,), jnp.float32, -2.5, 2.5), -2.5, 2.5),
        "tf_amps": gaussian(streams_of[5], (4, KNOTS), 1.5, 6.0, (), jnp.float32),
    }


bump_scale = 4.0


def over_blend(nearer, farther):
    return nearer + (1.0 - nearer[3:4]) * farther


def reference(owned_blocks, slot_counts, brick_order, view_flip, tf_centers, tf_amps):
    step_size = 1.5 / NZ
    brick_total = BX * BY * DB
    tile_lane = jnp.arange(N_TILE, dtype=jnp.int32)
    flip_column = jnp.repeat(view_flip, BX * BLOCK)
    partials = []
    for depth_row in range(N_DEPTH):
        counts = slot_counts[depth_row].astype(jnp.int32)
        order_row = brick_order[depth_row].astype(jnp.int32)
        starts = (jnp.cumsum(counts) - counts).astype(jnp.int32)
        position = jnp.sum(jnp.where(order_row[None, :] == tile_lane[:, None], tile_lane[None, :], 0), axis=1).astype(jnp.int32)
        local_index = jnp.arange(brick_total, dtype=jnp.int32)
        wanted = (local_index[None, :] * N_TILE + position[:, None]).astype(jnp.int32)
        owner_index = (jnp.sum((starts[None, None, :] <= wanted[:, :, None]).astype(jnp.int32), axis=2) - 1).astype(jnp.int32)
        slot_index = (owner_index * SLOTS + wanted - starts[owner_index]).astype(jnp.int32)
        blocks = owned_blocks[depth_row][slot_index.reshape(-1)]
        volume = blocks.reshape(N_TILE, DB, BY, BX, BLOCK, BLOCK, BLOCK).transpose(1, 4, 2, 5, 0, 3, 6)
        values = volume.reshape(DB * BLOCK, NY, NX).astype(jnp.float32)
        fields = [jnp.zeros_like(values) for channel in range(4)]
        for knot_index in range(KNOTS):
            bump_term = jnp.exp(-bump_scale * jnp.square(values - tf_centers[knot_index]))
            fields = [fields[channel] + tf_amps[channel, knot_index] * bump_term for channel in range(4)]
        extinction = jax.nn.softplus(fields[3])
        opacity_step = 1.0 - jnp.exp(-step_size * extinction)
        running = jnp.cumsum(extinction, axis=0)
        total = jnp.sum(extinction, axis=0)
        before = jnp.where(flip_column[None, None, :] == 1, total[None] - running, running - extinction)
        passed = jnp.exp(-step_size * before) * opacity_step
        colors = [jnp.sum(passed * jax.nn.sigmoid(fields[channel]), axis=0) for channel in range(3)]
        opacity = 1.0 - jnp.exp(-step_size * total)
        partials.append(jnp.stack(colors + [opacity], axis=0))
    rising = jnp.zeros((4, NY, NX), jnp.float32)
    for level_index in range(N_DEPTH - 1, -1, -1):
        rising = over_blend(partials[level_index], rising)
    falling = jnp.zeros((4, NY, NX), jnp.float32)
    for level_index in range(N_DEPTH):
        falling = over_blend(partials[level_index], falling)
    return jnp.where(flip_column[None, None, :] == 1, falling, rising)
```

```python
import functools
import math

import jax
import jax.numpy as jnp
from jax import lax
from jax.experimental import pallas as pl
from jax.experimental.pallas import tpu as pltpu
from jax.sharding import PartitionSpec as P

BLOCK = 32
BX = 4
BY = 4
DB = 2
KNOTS = 8
PIXELS = BLOCK * BLOCK
LANES = 128
TILES = PIXELS // LANES
BUMP_SCALE = 4.0
LOG2E = math.log2(math.e)
ROOT = math.sqrt(BUMP_SCALE * LOG2E)
CODE_TOP = 65535.0
CODE_MID = 32767.5
WIDE = 2


def exclusive_start(counts_ref, index, tile_count):
    start = jnp.int32(0)
    for i in range(tile_count):
        start = start + jnp.where(i < index, counts_ref[i], 0)
    return start


def position_of(order_ref, tile, tile_count):
    position = jnp.int32(0)
    for i in range(tile_count):
        position = position + jnp.where(order_ref[i] == tile, i, 0)
    return position


def encode(image):
    root = jnp.sqrt(jnp.sqrt(jnp.maximum(image, 0.0)))
    code = jnp.round(jnp.minimum(root, 1.0) * CODE_TOP - CODE_MID)
    return code.astype(jnp.int32).astype(jnp.int16)


def decode(code):
    root = (code.astype(jnp.int32).astype(jnp.float32) + CODE_MID) * (1.0 / CODE_TOP)
    square = root * root
    return square * square


def march_kernel(step_size, tile_count, relative, *refs):
    counts_ref, order_ref, flip_ref, me_ref, center_ref, amp_ref, cells_ref = refs[:7]
    outs = refs[7:7 + relative]
    coef_ref, stage_ref = refs[7 + relative:]
    step = pl.program_id(0)
    me = me_ref[0]
    start = exclusive_start(counts_ref, me, tile_count)
    live = counts_ref[me]

    @pl.when(step == 0)
    def _():
        w = center_ref[...] * ROOT
        folded = amp_ref[...] * jnp.exp2(-w * w)
        for k in range(KNOTS):
            coef_ref[k] = jnp.broadcast_to(2.0 * w[:, k:k + 1], (8, LANES))
            for c in range(4):
                scale = LOG2E if c == 3 else 0.5
                coef_ref[KNOTS + 4 * k + c] = jnp.broadcast_to(
                    folded[c:c + 1, k:k + 1] * scale, (8, LANES)
                )

    @pl.when(step * tile_count < live)
    def _():
        row = lax.broadcasted_iota(jnp.int32, (8, LANES), 0)
        for half in range(tile_count // 8):
            flip = jnp.zeros((8, LANES), jnp.int32)
            for s in range(8):
                tile = order_ref[lax.rem(start + half * 8 + s, tile_count)]
                flip = jnp.where(row == s, flip_ref[tile], flip)
            down = flip == 1
            signed_step = jnp.where(down, step_size * LOG2E, -step_size * LOG2E)

            def columns(group, carry, half=half, down=down, signed_step=signed_step):
                base = group * (WIDE * LANES)

                def depth(z, state):
                    lane = pl.multiple_of(z * PIXELS + base, LANES)
                    raw = cells_ref[half * 8:half * 8 + 8, pl.ds(lane, WIDE * LANES)]
                    values = raw.astype(jnp.float32) * ROOT
                    after = []
                    for j in range(WIDE):
                        v = values[:, j * LANES:(j + 1) * LANES]
                        total, seen, reds, greens, blues = state[j]
                        fields = [None] * 4
                        for k in range(KNOTS):
                            bump = jnp.exp2(v * (coef_ref[k] - v))
                            for c in range(4):
                                term = coef_ref[KNOTS + 4 * k + c] * bump
                                fields[c] = term if k == 0 else fields[c] + term
                        total = total + jnp.log(1.0 + jnp.exp2(fields[3]))
                        now = jnp.exp2(signed_step * total)
                        weight = now - seen
                        after.append((
                            total,
                            now,
                            reds + weight * jnp.tanh(fields[0]),
                            greens + weight * jnp.tanh(fields[1]),
                            blues + weight * jnp.tanh(fields[2]),
                        ))
                    return tuple(after)

                zero = jnp.zeros((8, LANES), jnp.float32)
                first = tuple((zero, zero + 1.0, zero, zero, zero) for j in range(WIDE))
                last = lax.fori_loop(0, BLOCK, depth, first)
                for j in range(WIDE):
                    total, seen, reds, greens, blues = last[j]
                    passed = jnp.exp2(total * (-step_size * LOG2E))
                    factor = jnp.where(down, 0.5 * passed, -0.5)
                    spread = seen - 1.0
                    rows = pl.ds(group * WIDE + j, 8, stride=TILES)
                    for c, color in enumerate((reds, greens, blues)):
                        stage_ref[half, c, rows, :] = factor * (spread + color)
                    stage_ref[half, 3, rows, :] = 1.0 - passed
                return carry

            lax.fori_loop(0, TILES // WIDE, columns, 0)
        for r in range(relative):
            tile = lax.rem(me + r, tile_count)
            slot = lax.rem(position_of(order_ref, tile, tile_count) - start + tile_count * 64, tile_count)
            rows = pl.ds(pl.multiple_of(lax.rem(slot, 8) * TILES, TILES), TILES)
            for c in range(4):
                outs[r][0, c] = encode(stage_ref[slot // 8, c, rows, :])


def march(counts, order, flip, me, centers, amps, cells, step_size):
    tile_count = counts.shape[0]
    slots = cells.shape[0]
    capacity = slots // tile_count
    scalar = pl.BlockSpec(memory_space=pltpu.SMEM)
    whole = lambda shape: pl.BlockSpec(shape, lambda m: (0,) * len(shape))
    block = pl.BlockSpec((1, 4, TILES, LANES), lambda m: (m, 0, 0, 0))
    return pl.pallas_call(
        functools.partial(march_kernel, step_size, tile_count, tile_count),
        grid=(capacity,),
        in_specs=[scalar] * 4 + [
            whole((1, KNOTS)),
            whole((4, KNOTS)),
            pl.BlockSpec((tile_count, cells.shape[1]), lambda m: (m, 0)),
        ],
        out_specs=[block] * tile_count,
        out_shape=[jax.ShapeDtypeStruct((capacity, 4, TILES, LANES), jnp.int16)] * tile_count,
        scratch_shapes=[
            pltpu.VMEM((KNOTS * 5, 8, LANES), jnp.float32),
            pltpu.VMEM((tile_count // 8, 4, 8 * TILES, LANES), jnp.float32),
        ],
        name="march",
    )(counts, order, flip, me, centers.reshape(1, KNOTS), amps, cells)


def over(nearer, farther, uncovered):
    return nearer + uncovered * farther


def gather_kernel(tile_count, capacity, *refs):
    counts_ref, order_ref, flip_ref, me_ref = refs[:4]
    arrived = refs[4:4 + tile_count]
    out_ref, brick_ref = refs[4 + tile_count:]
    me = me_ref[0]
    position = position_of(order_ref, me, tile_count)
    for r in range(tile_count):
        owner = lax.rem(me - r + tile_count, tile_count)
        start = exclusive_start(counts_ref, owner, tile_count)
        offset = lax.rem(position - start + tile_count * 64, tile_count)
        level = (start + offset - position) // tile_count
        held = (counts_ref[owner] - offset + tile_count - 1) // tile_count

        def place(m, carry, r=r, level=level):
            for c in range(4):
                brick_ref[level + m, c] = decode(arrived[r][m, c])
            return carry

        lax.fori_loop(0, held, place, 0)
    flip = flip_ref[me] == 1
    lane = lax.broadcasted_iota(jnp.int32, (TILES, LANES), 1) // BLOCK
    per_row = LANES // BLOCK
    for by in range(BY):
        images = []
        for bx in range(BX):
            layers = [(bz * BY + by) * BX + bx for bz in range(DB)]
            parts = None
            for n in range(DB):
                index = jnp.where(flip, layers[n], layers[DB - 1 - n])
                new = [brick_ref[index, c] for c in range(4)]
                if parts is None:
                    parts = new
                else:
                    uncovered = 1.0 - new[3]
                    parts = [new[c] + uncovered * parts[c] for c in range(4)]
            images.append(parts)
        for c in range(4):
            for s in range(per_row):
                line = None
                for bx in range(BX):
                    turn = (bx - s) * BLOCK % LANES
                    moved = images[bx][c]
                    if turn:
                        moved = pltpu.roll(moved, turn, 1)
                    line = moved if line is None else jnp.where(lane == bx, moved, line)
                out_ref[c, pl.ds(by * BLOCK + s, TILES, stride=per_row), :] = line


def gather(counts, order, flip, me, arrived):
    tile_count = counts.shape[0]
    capacity = arrived[0].shape[0]
    scalar = pl.BlockSpec(memory_space=pltpu.SMEM)
    vmem = pl.BlockSpec(memory_space=pltpu.VMEM)
    return pl.pallas_call(
        functools.partial(gather_kernel, tile_count, capacity),
        in_specs=[scalar] * 4 + [vmem] * tile_count,
        out_specs=vmem,
        out_shape=jax.ShapeDtypeStruct((4, BY * BLOCK, BX * BLOCK), jnp.float32),
        scratch_shapes=[pltpu.VMEM((DB * BY * BX, 4, TILES, LANES), jnp.float32)],
        name="gather",
    )(counts, order, flip, me, *arrived)


def over_blend(nearer, farther, chan_axis):
    coverage = lax.slice_in_dim(nearer, 3, 4, axis=chan_axis)
    return nearer + (1.0 - coverage) * farther


def swapped(block, axis, bit):
    count = lax.axis_size(axis)
    return lax.ppermute(block, axis, [(i, i ^ 1 << bit) for i in range(count)])


def body(owned_blocks, slot_counts, brick_order, view_flip, tf_centers, tf_amps):
    tile_count = lax.axis_size("tile")
    depth_count = lax.axis_size("depth")
    depth_index = lax.axis_index("depth")
    step_size = 1.5 / (depth_count * DB * BLOCK)
    me = lax.axis_index("tile").astype(jnp.int32).reshape(1)
    counts, order = slot_counts[0], brick_order[0]
    sent = march(counts, order, view_flip, me, tf_centers, tf_amps, owned_blocks[0], step_size)
    arrived = [sent[0]]
    for r in range(1, tile_count):
        route = [(i, (i + r) % tile_count) for i in range(tile_count)]
        arrived.append(lax.ppermute(sent[r], "tile", route))
    tile_image = gather(counts, order, view_flip, me, arrived)
    flip_mine = jnp.sum(jnp.where(jnp.arange(tile_count, dtype=jnp.int32) == me[0], view_flip, 0))
    levels = depth_count.bit_length() - 1
    row_share = tile_image.shape[1] // depth_count
    width = tile_image.shape[2]
    current = tile_image.reshape((4,) + (2,) * levels + (row_share, width))
    for bit_index in range(levels):
        split_axis = 1 + (levels - 1 - bit_index)
        lower_half = lax.slice_in_dim(current, 0, 1, axis=split_axis)
        upper_half = lax.slice_in_dim(current, 1, 2, axis=split_axis)
        high_side = depth_index >> bit_index & 1
        kept_half = jnp.where(high_side == 1, upper_half, lower_half)
        given_half = jnp.where(high_side == 1, lower_half, upper_half)
        other_half = swapped(given_half, "depth", bit_index)
        mine_front = high_side == flip_mine
        current = jnp.where(
            mine_front, over_blend(kept_half, other_half, 0), over_blend(other_half, kept_half, 0)
        )
    return current.reshape(4, row_share, width)


def solution(mesh):
    in_specs = (P("depth", "tile", None), P("depth", None), P("depth", None), P(), P(), P())
    out_specs = P(None, "depth", "tile")
    return jax.shard_map(body, mesh=mesh, in_specs=in_specs, out_specs=out_specs, check_vma=False)
```

```python
import functools
import math

import jax
import jax.numpy as jnp
from jax import lax
from jax.experimental import pallas as pl
from jax.experimental.pallas import tpu as pltpu
from jax.sharding import PartitionSpec as P

BLOCK = 32
BX = 4
BY = 4
DB = 2
KNOTS = 8
PIXELS = BLOCK * BLOCK
LANES = 128
TILES = PIXELS // LANES
BUMP_SCALE = 4.0
LOG2E = math.log2(math.e)
ROOT = math.sqrt(BUMP_SCALE * LOG2E)
CODE_TOP = 65535.0
CODE_MID = 32767.5
WIDE = 2
UNROLL = 16


def exclusive_start(counts_ref, index, tile_count):
    start = jnp.int32(0)
    for i in range(tile_count):
        start = start + jnp.where(i < index, counts_ref[i], 0)
    return start


def position_of(order_ref, tile, tile_count):
    position = jnp.int32(0)
    for i in range(tile_count):
        position = position + jnp.where(order_ref[i] == tile, i, 0)
    return position


def encode(image):
    root = jnp.exp2(jnp.log(jnp.maximum(image, 0.0)) * (0.25 * LOG2E))
    code = jnp.round(jnp.minimum(root, 1.0) * CODE_TOP - CODE_MID)
    return code.astype(jnp.int32).astype(jnp.int16)


def decode(code):
    root = (code.astype(jnp.int32).astype(jnp.float32) + CODE_MID) * (1.0 / CODE_TOP)
    square = root * root
    return square * square


def march_kernel(step_size, tile_count, relative, *refs):
    counts_ref, order_ref, flip_ref, me_ref, center_ref, amp_ref, cells_ref = refs[:7]
    outs = refs[7:7 + relative]
    coef_ref, stage_ref = refs[7 + relative:]
    step = pl.program_id(0)
    me = me_ref[0]
    start = exclusive_start(counts_ref, me, tile_count)
    live = counts_ref[me]

    @pl.when(step == 0)
    def _():
        w = center_ref[...] * ROOT
        folded = amp_ref[...] * jnp.exp2(-w * w)
        for k in range(KNOTS):
            coef_ref[k] = jnp.broadcast_to(2.0 * w[:, k:k + 1], (8, LANES))
            for c in range(4):
                scale = LOG2E if c == 3 else 0.5
                coef_ref[KNOTS + 4 * k + c] = jnp.broadcast_to(
                    folded[c:c + 1, k:k + 1] * scale, (8, LANES)
                )

    @pl.when(step * tile_count < live)
    def _():
        row = lax.broadcasted_iota(jnp.int32, (8, LANES), 0)
        for half in range(tile_count // 8):
            flip = jnp.zeros((8, LANES), jnp.int32)
            for s in range(8):
                tile = order_ref[lax.rem(start + half * 8 + s, tile_count)]
                flip = jnp.where(row == s, flip_ref[tile], flip)
            down = flip == 1
            signed_step = jnp.where(down, step_size * LOG2E, -step_size * LOG2E)

            def columns(group, carry, half=half, down=down, signed_step=signed_step):
                base = group * (WIDE * LANES)

                def depth(z, state):
                    lane = pl.multiple_of(z * PIXELS + base, LANES)
                    raw = cells_ref[half * 8:half * 8 + 8, pl.ds(lane, WIDE * LANES)]
                    values = raw.astype(jnp.float32) * ROOT
                    after = []
                    for j in range(WIDE):
                        v = values[:, j * LANES:(j + 1) * LANES]
                        total, seen, reds, greens, blues = state[j]
                        fields = [None] * 4
                        for k in range(KNOTS):
                            bump = jnp.exp2(v * (coef_ref[k] - v))
                            for c in range(4):
                                term = coef_ref[KNOTS + 4 * k + c] * bump
                                fields[c] = term if k == 0 else fields[c] + term
                        total = total + jnp.log(1.0 + jnp.exp2(fields[3]))
                        now = jnp.exp2(signed_step * total)
                        weight = now - seen
                        after.append((
                            total,
                            now,
                            reds + weight * jnp.tanh(fields[0]),
                            greens + weight * jnp.tanh(fields[1]),
                            blues + weight * jnp.tanh(fields[2]),
                        ))
                    return tuple(after)

                zero = jnp.zeros((8, LANES), jnp.float32)
                first = tuple((zero, zero + 1.0, zero, zero, zero) for j in range(WIDE))
                last = lax.fori_loop(0, BLOCK, depth, first, unroll=UNROLL)
                for j in range(WIDE):
                    total, seen, reds, greens, blues = last[j]
                    passed = jnp.exp2(total * (-step_size * LOG2E))
                    factor = jnp.where(down, 0.5 * passed, -0.5)
                    spread = seen - 1.0
                    rows = pl.ds(group * WIDE + j, 8, stride=TILES)
                    for c, color in enumerate((reds, greens, blues)):
                        stage_ref[half, c, rows, :] = factor * (spread + color)
                    stage_ref[half, 3, rows, :] = 1.0 - passed
                return carry

            lax.fori_loop(0, TILES // WIDE, columns, 0)
        for r in range(relative):
            tile = lax.rem(me + r, tile_count)
            slot = lax.rem(position_of(order_ref, tile, tile_count) - start + tile_count * 64, tile_count)
            rows = pl.ds(pl.multiple_of(lax.rem(slot, 8) * TILES, TILES), TILES)
            for c in range(4):
                outs[r][0, c] = encode(stage_ref[slot // 8, c, rows, :])


def march(counts, order, flip, me, centers, amps, cells, step_size):
    tile_count = counts.shape[0]
    slots = cells.shape[0]
    capacity = slots // tile_count
    scalar = pl.BlockSpec(memory_space=pltpu.SMEM)
    whole = lambda shape: pl.BlockSpec(shape, lambda m: (0,) * len(shape))
    block = pl.BlockSpec((1, 4, TILES, LANES), lambda m: (m, 0, 0, 0))
    return pl.pallas_call(
        functools.partial(march_kernel, step_size, tile_count, tile_count),
        grid=(capacity,),
        in_specs=[scalar] * 4 + [
            whole((1, KNOTS)),
            whole((4, KNOTS)),
            pl.BlockSpec((tile_count, cells.shape[1]), lambda m: (m, 0)),
        ],
        out_specs=[block] * tile_count,
        out_shape=[jax.ShapeDtypeStruct((capacity, 4, TILES, LANES), jnp.int16)] * tile_count,
        scratch_shapes=[
            pltpu.VMEM((KNOTS * 5, 8, LANES), jnp.float32),
            pltpu.VMEM((tile_count // 8, 4, 8 * TILES, LANES), jnp.float32),
        ],
        name="march",
    )(counts, order, flip, me, centers.reshape(1, KNOTS), amps, cells)


def over(nearer, farther, uncovered):
    return nearer + uncovered * farther


def gather_kernel(tile_count, capacity, *refs):
    counts_ref, order_ref, flip_ref, me_ref = refs[:4]
    arrived = refs[4:4 + tile_count]
    out_ref, brick_ref = refs[4 + tile_count:]
    me = me_ref[0]
    position = position_of(order_ref, me, tile_count)
    for r in range(tile_count):
        owner = lax.rem(me - r + tile_count, tile_count)
        start = exclusive_start(counts_ref, owner, tile_count)
        offset = lax.rem(position - start + tile_count * 64, tile_count)
        level = (start + offset - position) // tile_count
        held = (counts_ref[owner] - offset + tile_count - 1) // tile_count

        def place(m, carry, r=r, level=level):
            for c in range(4):
                brick_ref[level + m, c] = decode(arrived[r][m, c])
            return carry

        lax.fori_loop(0, held, place, 0)
    flip = flip_ref[me] == 1
    lane = lax.broadcasted_iota(jnp.int32, (TILES, LANES), 1) // BLOCK
    per_row = LANES // BLOCK
    for by in range(BY):
        images = []
        for bx in range(BX):
            layers = [(bz * BY + by) * BX + bx for bz in range(DB)]
            parts = None
            for n in range(DB):
                index = jnp.where(flip, layers[n], layers[DB - 1 - n])
                new = [brick_ref[index, c] for c in range(4)]
                if parts is None:
                    parts = new
                else:
                    uncovered = 1.0 - new[3]
                    parts = [new[c] + uncovered * parts[c] for c in range(4)]
            images.append(parts)
        for c in range(4):
            for s in range(per_row):
                line = None
                for bx in range(BX):
                    turn = (bx - s) * BLOCK % LANES
                    moved = images[bx][c]
                    if turn:
                        moved = pltpu.roll(moved, turn, 1)
                    line = moved if line is None else jnp.where(lane == bx, moved, line)
                out_ref[c, pl.ds(by * BLOCK + s, TILES, stride=per_row), :] = line


def gather(counts, order, flip, me, arrived):
    tile_count = counts.shape[0]
    capacity = arrived[0].shape[0]
    scalar = pl.BlockSpec(memory_space=pltpu.SMEM)
    vmem = pl.BlockSpec(memory_space=pltpu.VMEM)
    return pl.pallas_call(
        functools.partial(gather_kernel, tile_count, capacity),
        in_specs=[scalar] * 4 + [vmem] * tile_count,
        out_specs=vmem,
        out_shape=jax.ShapeDtypeStruct((4, BY * BLOCK, BX * BLOCK), jnp.float32),
        scratch_shapes=[pltpu.VMEM((DB * BY * BX, 4, TILES, LANES), jnp.float32)],
        name="gather",
    )(counts, order, flip, me, *arrived)


def over_blend(nearer, farther, chan_axis):
    coverage = lax.slice_in_dim(nearer, 3, 4, axis=chan_axis)
    return nearer + (1.0 - coverage) * farther


def swapped(block, axis, bit):
    count = lax.axis_size(axis)
    return lax.ppermute(block, axis, [(i, i ^ 1 << bit) for i in range(count)])


def body(owned_blocks, slot_counts, brick_order, view_flip, tf_centers, tf_amps):
    tile_count = lax.axis_size("tile")
    depth_count = lax.axis_size("depth")
    depth_index = lax.axis_index("depth")
    step_size = 1.5 / (depth_count * DB * BLOCK)
    me = lax.axis_index("tile").astype(jnp.int32).reshape(1)
    counts, order = slot_counts[0], brick_order[0]
    sent = march(counts, order, view_flip, me, tf_centers, tf_amps, owned_blocks[0], step_size)
    arrived = [sent[0]]
    for r in range(1, tile_count):
        route = [(i, (i + r) % tile_count) for i in range(tile_count)]
        arrived.append(lax.ppermute(sent[r], "tile", route))
    tile_image = gather(counts, order, view_flip, me, arrived)
    flip_mine = jnp.sum(jnp.where(jnp.arange(tile_count, dtype=jnp.int32) == me[0], view_flip, 0))
    levels = depth_count.bit_length() - 1
    row_share = tile_image.shape[1] // depth_count
    width = tile_image.shape[2]
    current = tile_image.reshape((4,) + (2,) * levels + (row_share, width))
    for bit_index in range(levels):
        split_axis = 1 + (levels - 1 - bit_index)
        lower_half = lax.slice_in_dim(current, 0, 1, axis=split_axis)
        upper_half = lax.slice_in_dim(current, 1, 2, axis=split_axis)
        high_side = depth_index >> bit_index & 1
        kept_half = jnp.where(high_side == 1, upper_half, lower_half)
        given_half = jnp.where(high_side == 1, lower_half, upper_half)
        other_half = swapped(given_half, "depth", bit_index)
        mine_front = high_side == flip_mine
        current = jnp.where(
            mine_front, over_blend(kept_half, other_half, 0), over_blend(other_half, kept_half, 0)
        )
    return current.reshape(4, row_share, width)


def solution(mesh):
    in_specs = (P("depth", "tile", None), P("depth", None), P("depth", None), P(), P(), P())
    out_specs = P(None, "depth", "tile")
    return jax.shard_map(body, mesh=mesh, in_specs=in_specs, out_specs=out_specs, check_vma=False)
```

```python
import functools
import math

import jax
import jax.numpy as jnp
from jax import lax
from jax.experimental import pallas as pl
from jax.experimental.pallas import tpu as pltpu
from jax.sharding import PartitionSpec as P

BLOCK = 32
BX = 4
BY = 4
DB = 2
KNOTS = 8
PIXELS = BLOCK * BLOCK
LANES = 128
TILES = PIXELS // LANES
BUMP_SCALE = 4.0
LOG2E = math.log2(math.e)
ROOT = math.sqrt(BUMP_SCALE * LOG2E)
CODE_TOP = 65535.0
CODE_MID = 32767.5
GRANT = 12 << 20
MARCH_GRANT = 61 << 20
WIDE = 2
UNROLL = 16


def exclusive_start(counts_ref, index, tile_count):
    start = jnp.int32(0)
    for i in range(tile_count):
        start = start + jnp.where(i < index, counts_ref[i], 0)
    return start


def position_of(order_ref, tile, tile_count):
    position = jnp.int32(0)
    for i in range(tile_count):
        position = position + jnp.where(order_ref[i] == tile, i, 0)
    return position


def encode(image):
    root = jnp.exp2(jnp.log(jnp.maximum(image, 0.0)) * (0.25 * LOG2E))
    code = jnp.round(jnp.minimum(root, 1.0) * CODE_TOP - CODE_MID)
    return code.astype(jnp.int32).astype(jnp.int16)


def decode(code):
    root = (code.astype(jnp.int32).astype(jnp.float32) + CODE_MID) * (1.0 / CODE_TOP)
    square = root * root
    return square * square


def march_kernel(step_size, tile_count, relative, *refs):
    counts_ref, order_ref, flip_ref, me_ref, center_ref, amp_ref, cells_ref = refs[:7]
    outs = refs[7:7 + relative]
    coef_ref, stage_ref = refs[7 + relative:]
    step = pl.program_id(0)
    me = me_ref[0]
    start = exclusive_start(counts_ref, me, tile_count)
    live = counts_ref[me]

    @pl.when(step == 0)
    def _():
        w = center_ref[...] * ROOT
        folded = amp_ref[...] * jnp.exp2(-w * w)
        for k in range(KNOTS):
            coef_ref[k] = jnp.broadcast_to(2.0 * w[:, k:k + 1], (8, LANES))
            for c in range(4):
                scale = LOG2E if c == 3 else 0.5
                coef_ref[KNOTS + 4 * k + c] = jnp.broadcast_to(
                    folded[c:c + 1, k:k + 1] * scale, (8, LANES)
                )

    @pl.when(step * tile_count < live)
    def _():
        row = lax.broadcasted_iota(jnp.int32, (8, LANES), 0)
        for half in range(tile_count // 8):
            flip = jnp.zeros((8, LANES), jnp.int32)
            for s in range(8):
                tile = order_ref[lax.rem(start + half * 8 + s, tile_count)]
                flip = jnp.where(row == s, flip_ref[tile], flip)
            down = flip == 1
            signed_step = jnp.where(down, step_size * LOG2E, -step_size * LOG2E)

            def columns(group, carry, half=half, down=down, signed_step=signed_step):
                base = group * (WIDE * LANES)

                def depth(z, state):
                    lane = pl.multiple_of(z * PIXELS + base, LANES)
                    raw = cells_ref[half * 8:half * 8 + 8, pl.ds(lane, WIDE * LANES)]
                    values = raw.astype(jnp.float32) * ROOT
                    after = []
                    for j in range(WIDE):
                        v = values[:, j * LANES:(j + 1) * LANES]
                        total, seen, reds, greens, blues = state[j]
                        fields = [None] * 4
                        for k in range(KNOTS):
                            bump = jnp.exp2(v * (coef_ref[k] - v))
                            for c in range(4):
                                term = coef_ref[KNOTS + 4 * k + c] * bump
                                fields[c] = term if k == 0 else fields[c] + term
                        total = total + jnp.log(1.0 + jnp.exp2(fields[3]))
                        now = jnp.exp2(signed_step * total)
                        weight = now - seen
                        after.append((
                            total,
                            now,
                            reds + weight * jnp.tanh(fields[0]),
                            greens + weight * jnp.tanh(fields[1]),
                            blues + weight * jnp.tanh(fields[2]),
                        ))
                    return tuple(after)

                zero = jnp.zeros((8, LANES), jnp.float32)
                first = tuple((zero, zero + 1.0, zero, zero, zero) for j in range(WIDE))
                last = lax.fori_loop(0, BLOCK, depth, first, unroll=UNROLL)
                for j in range(WIDE):
                    total, seen, reds, greens, blues = last[j]
                    passed = jnp.exp2(total * (-step_size * LOG2E))
                    factor = jnp.where(down, 0.5 * passed, -0.5)
                    spread = seen - 1.0
                    rows = pl.ds(group * WIDE + j, 8, stride=TILES)
                    for c, color in enumerate((reds, greens, blues)):
                        stage_ref[half, c, rows, :] = factor * (spread + color)
                    stage_ref[half, 3, rows, :] = 1.0 - passed
                return carry

            lax.fori_loop(0, TILES // WIDE, columns, 0)
        for r in range(relative):
            tile = lax.rem(me + r, tile_count)
            slot = lax.rem(position_of(order_ref, tile, tile_count) - start + tile_count * 64, tile_count)
            rows = pl.ds(pl.multiple_of(lax.rem(slot, 8) * TILES, TILES), TILES)
            for c in range(4):
                outs[r][0, c] = encode(stage_ref[slot // 8, c, rows, :])


def march(counts, order, flip, me, centers, amps, cells, step_size):
    tile_count = counts.shape[0]
    slots = cells.shape[0]
    capacity = slots // tile_count
    scalar = pl.BlockSpec(memory_space=pltpu.SMEM)
    whole = lambda shape: pl.BlockSpec(shape, lambda m: (0,) * len(shape))
    block = pl.BlockSpec((1, 4, TILES, LANES), lambda m: (m, 0, 0, 0))
    return pl.pallas_call(
        functools.partial(march_kernel, step_size, tile_count, tile_count),
        grid=(capacity,),
        in_specs=[scalar] * 4 + [
            whole((1, KNOTS)),
            whole((4, KNOTS)),
            pl.BlockSpec((tile_count, cells.shape[1]), lambda m: (m, 0)),
        ],
        out_specs=[block] * tile_count,
        out_shape=[jax.ShapeDtypeStruct((capacity, 4, TILES, LANES), jnp.int16)] * tile_count,
        scratch_shapes=[
            pltpu.VMEM((KNOTS * 5, 8, LANES), jnp.float32),
            pltpu.VMEM((tile_count // 8, 4, 8 * TILES, LANES), jnp.float32),
        ],
        compiler_params=pltpu.CompilerParams(vmem_limit_bytes=MARCH_GRANT),
        name="march",
    )(counts, order, flip, me, centers.reshape(1, KNOTS), amps, cells)


def split_rows(image, kept_ref, given_ref, low, row_share):
    for n in range(kept_ref.shape[1] // row_share):
        mine = pl.multiple_of((2 * n + low) * row_share, row_share)
        theirs = pl.multiple_of((2 * n + 1 - low) * row_share, row_share)
        for c in range(4):
            kept_ref[c, n * row_share:(n + 1) * row_share] = image[c, pl.ds(mine, row_share)]
            given_ref[c, n * row_share:(n + 1) * row_share] = image[c, pl.ds(theirs, row_share)]


def gather_kernel(tile_count, row_share, *refs):
    counts_ref, order_ref, flip_ref, me_ref = refs[:4]
    arrived = refs[4:4 + tile_count]
    kept_ref, given_ref, brick_ref, image_ref = refs[4 + tile_count:]
    me = me_ref[0]
    position = position_of(order_ref, me, tile_count)
    starts = [jnp.int32(0)]
    for i in range(tile_count):
        starts.append(starts[-1] + counts_ref[i])
    for r in range(tile_count):
        owner = lax.rem(me - r + tile_count, tile_count)
        start = jnp.int32(0)
        for i in range(tile_count):
            start = jnp.where(owner == i, starts[i], start)
        offset = lax.rem(position - start + tile_count * 64, tile_count)
        level = (start + offset - position) // tile_count
        held = (counts_ref[owner] - offset + tile_count - 1) // tile_count

        def place(m, carry, r=r, level=level):
            brick_ref[level + m] = decode(arrived[r][m])
            return carry

        lax.fori_loop(0, held, place, 0)
    flip = flip_ref[me] == 1
    lane = lax.broadcasted_iota(jnp.int32, (TILES, LANES), 1) // BLOCK
    per_row = LANES // BLOCK
    for by in range(BY):
        images = []
        for bx in range(BX):
            layers = [(bz * BY + by) * BX + bx for bz in range(DB)]
            parts = None
            for n in range(DB):
                index = jnp.where(flip, layers[n], layers[DB - 1 - n])
                new = [brick_ref[index, c] for c in range(4)]
                if parts is None:
                    parts = new
                else:
                    uncovered = 1.0 - new[3]
                    parts = [new[c] + uncovered * parts[c] for c in range(4)]
            images.append(parts)
        for c in range(4):
            for s in range(per_row):
                line = None
                for bx in range(BX):
                    turn = (bx - s) * BLOCK % LANES
                    moved = images[bx][c]
                    if turn:
                        moved = pltpu.roll(moved, turn, 1)
                    line = moved if line is None else jnp.where(lane == bx, moved, line)
                image_ref[c, pl.ds(by * BLOCK + s, TILES, stride=per_row), :] = line
    split_rows(image_ref, kept_ref, given_ref, me_ref[1] & 1, row_share)


def gather(counts, order, flip, me, arrived, row_share):
    tile_count = counts.shape[0]
    scalar = pl.BlockSpec(memory_space=pltpu.SMEM)
    vmem = pl.BlockSpec(memory_space=pltpu.VMEM)
    rows, width = BY * BLOCK, BX * BLOCK
    half = jax.ShapeDtypeStruct((4, rows // 2, width), jnp.float32)
    return pl.pallas_call(
        functools.partial(gather_kernel, tile_count, row_share),
        in_specs=[scalar] * 4 + [vmem] * tile_count,
        out_specs=[vmem] * 2,
        out_shape=[half, half],
        scratch_shapes=[
            pltpu.VMEM((DB * BY * BX, 4, TILES, LANES), jnp.float32),
            pltpu.VMEM((4, rows, width), jnp.float32),
        ],
        compiler_params=pltpu.CompilerParams(vmem_limit_bytes=GRANT),
        name="gather",
    )(counts, order, flip, me, *arrived)


def blend_kernel(bit, row_share, *refs):
    flip_ref, me_ref, kept_ref, other_ref = refs[:4]
    side = me_ref[1] >> bit & 1
    front = side == flip_ref[me_ref[0]]
    last = len(refs) == 5
    out_ref = refs[-1]

    def blend(near_ref, far_ref):
        uncovered = 1.0 - near_ref[3]
        for c in range(4):
            out_ref[c] = near_ref[c] + uncovered * far_ref[c]

    @pl.when(front)
    def _():
        blend(kept_ref, other_ref)

    @pl.when(jnp.logical_not(front))
    def _():
        blend(other_ref, kept_ref)

    if not last:
        split_rows(out_ref, refs[4], refs[5], me_ref[1] >> (bit + 1) & 1, row_share)


def blend(flip, me, kept, other, bit, row_share):
    scalar = pl.BlockSpec(memory_space=pltpu.SMEM)
    vmem = pl.BlockSpec(memory_space=pltpu.VMEM)
    last = kept.shape[1] == row_share
    whole = jax.ShapeDtypeStruct(kept.shape, jnp.float32)
    half = jax.ShapeDtypeStruct((4, kept.shape[1] // 2, kept.shape[2]), jnp.float32)
    return pl.pallas_call(
        functools.partial(blend_kernel, bit, row_share),
        in_specs=[scalar] * 2 + [vmem] * 2,
        out_specs=vmem if last else [vmem] * 2,
        out_shape=whole if last else [half, half],
        scratch_shapes=[] if last else [pltpu.VMEM(kept.shape, jnp.float32)],
        compiler_params=pltpu.CompilerParams(vmem_limit_bytes=GRANT),
        name="blend",
    )(flip, me, kept, other)


def swapped(block, axis, bit):
    count = lax.axis_size(axis)
    return lax.ppermute(block, axis, [(i, i ^ 1 << bit) for i in range(count)])


def body(owned_blocks, slot_counts, brick_order, view_flip, tf_centers, tf_amps):
    tile_count = lax.axis_size("tile")
    depth_count = lax.axis_size("depth")
    step_size = 1.5 / (depth_count * DB * BLOCK)
    me = jnp.stack([lax.axis_index("tile"), lax.axis_index("depth")]).astype(jnp.int32)
    counts, order = slot_counts[0], brick_order[0]
    sent = march(counts, order, view_flip, me, tf_centers, tf_amps, owned_blocks[0], step_size)
    arrived = [sent[0]]
    for r in range(1, tile_count):
        route = [(i, (i + r) % tile_count) for i in range(tile_count)]
        arrived.append(lax.ppermute(sent[r], "tile", route))
    row_share = BY * BLOCK // depth_count
    kept, given = gather(counts, order, view_flip, me, arrived, row_share)
    levels = depth_count.bit_length() - 1
    for bit in range(levels):
        other = swapped(given, "depth", bit)
        blended = blend(view_flip, me, kept, other, bit, row_share)
        if bit < levels - 1:
            kept, given = blended
    return blended


def solution(mesh):
    in_specs = (P("depth", "tile", None), P("depth", None), P("depth", None), P(), P(), P())
    out_specs = P(None, "depth", "tile")
    return jax.shard_map(body, mesh=mesh, in_specs=in_specs, out_specs=out_specs, check_vma=False)
```

```python
import functools
import math

import jax
import jax.numpy as jnp
from jax import lax
from jax.experimental import pallas as pl
from jax.experimental.pallas import tpu as pltpu
from jax.sharding import PartitionSpec as P

BLOCK = 32
BX = 4
BY = 4
DB = 2
KNOTS = 8
PIXELS = BLOCK * BLOCK
LANES = 128
TILES = PIXELS // LANES
BUMP_SCALE = 4.0
LOG2E = math.log2(math.e)
ROOT = math.sqrt(BUMP_SCALE * LOG2E)
CODE_TOP = 65535.0
CODE_MID = 32767.5
GRANT = 12 << 20
MARCH_GRANT = 61 << 20
SPAN = 1024
GROUPS = PIXELS // SPAN
STACK = 8 * GROUPS
PACK = 16 // 8


def exclusive_start(counts_ref, index, tile_count):
    start = jnp.int32(0)
    for i in range(tile_count):
        start = start + jnp.where(i < index, counts_ref[i], 0)
    return start


def position_of(order_ref, tile, tile_count):
    position = jnp.int32(0)
    for i in range(tile_count):
        position = position + jnp.where(order_ref[i] == tile, i, 0)
    return position


def encode(image):
    root = jnp.exp2(jnp.log(jnp.maximum(image, 0.0)) * (0.25 * LOG2E))
    code = jnp.round(jnp.minimum(root, 1.0) * CODE_TOP - CODE_MID)
    return code.astype(jnp.int32).astype(jnp.int16)


def decode(code):
    root = (code.astype(jnp.int32).astype(jnp.float32) + CODE_MID) * (1.0 / CODE_TOP)
    square = root * root
    return square * square


def march_kernel(step_size, tile_count, relative, *refs):
    counts_ref, order_ref, flip_ref, me_ref, center_ref, amp_ref, cells_ref = refs[:7]
    outs = refs[7:7 + relative]
    coef_ref, mix_ref, stage_ref, slot_ref = refs[7 + relative:]
    step = pl.program_id(0)
    me = me_ref[0]
    start = exclusive_start(counts_ref, me, tile_count)
    live = counts_ref[me]

    @pl.when(step == 0)
    def _():
        for r in range(relative):
            tile = lax.rem(me + r, tile_count)
            slot_ref[r] = lax.rem(
                position_of(order_ref, tile, tile_count) - start + tile_count * 64, tile_count
            )
        w = center_ref[...] * ROOT
        folded = amp_ref[...] * jnp.exp2(-w * w)
        channel = lax.broadcasted_iota(jnp.int32, (4, 1), 0)
        folded = folded * jnp.where(channel == 3, LOG2E, 0.5)
        for k in range(KNOTS):
            coef_ref[k] = jnp.broadcast_to(2.0 * w[:, k:k + 1], (8, LANES))
        knot = lax.broadcasted_iota(jnp.int32, (4, KNOTS * STACK), 1) // STACK
        spread = jnp.zeros((4, KNOTS * STACK), jnp.float32)
        for k in range(KNOTS):
            spread = jnp.where(knot == k, folded[:, k:k + 1], spread)
        coarse = spread.astype(jnp.bfloat16)
        fine = (spread - coarse.astype(jnp.float32)).astype(jnp.bfloat16)
        own = lax.broadcasted_iota(jnp.int32, (STACK, KNOTS * STACK), 0) == lax.rem(
            lax.broadcasted_iota(jnp.int32, (STACK, KNOTS * STACK), 1), STACK
        )
        width = KNOTS * STACK
        for part, amps in enumerate((coarse, fine, coarse)):
            amps = amps.astype(jnp.float32)
            for c in range(4):
                line = jnp.where(own, amps[c:c + 1], 0.0)
                mix_ref[c * STACK:(c + 1) * STACK, part * width:(part + 1) * width] = line.astype(jnp.bfloat16)

    @pl.when(step * tile_count < live)
    def _():
        row = lax.broadcasted_iota(jnp.int32, (8, SPAN), 0)
        for half in range(tile_count // 8):
            flip = jnp.zeros((8, SPAN), jnp.int32)
            for s in range(8):
                tile = order_ref[lax.rem(start + half * 8 + s, tile_count)]
                flip = jnp.where(row == s, flip_ref[tile], flip)
            down = flip == 1
            signed_step = jnp.where(down, step_size * LOG2E, -step_size * LOG2E)

            def depth(z, state, half=half, signed_step=signed_step):
                values = []
                for j in range(GROUPS):
                    lane = pl.multiple_of(z * PIXELS + j * SPAN, LANES)
                    raw = cells_ref[half * 8:half * 8 + 8, pl.ds(lane, SPAN)]
                    values.append(raw.astype(jnp.float32) * ROOT)
                bumps = []
                for k in range(KNOTS):
                    center = jnp.concatenate([coef_ref[k]] * (SPAN // LANES), axis=1)
                    bumps += [jnp.exp2(v * (center - v)) for v in values]
                high, low = [], []
                for n in range(0, len(bumps), PACK):
                    bump = jnp.concatenate(bumps[n:n + PACK], axis=0)
                    coarse = bump.astype(jnp.bfloat16)
                    high.append(coarse)
                    low.append((bump - coarse.astype(jnp.float32)).astype(jnp.bfloat16))
                stacked = jnp.concatenate(high + high + low, axis=0)
                fields = jnp.dot(mix_ref[...], stacked, preferred_element_type=jnp.float32)
                after = []
                for j in range(GROUPS):
                    red, green, blue, dense = (
                        fields[c * STACK + j * 8:c * STACK + j * 8 + 8] for c in range(4)
                    )
                    total, seen, reds, greens, blues = state[j]
                    total = total + jnp.log(1.0 + jnp.exp2(dense))
                    now = jnp.exp2(signed_step * total)
                    weight = now - seen
                    after.append((
                        total,
                        now,
                        reds + weight * jnp.tanh(red),
                        greens + weight * jnp.tanh(green),
                        blues + weight * jnp.tanh(blue),
                    ))
                return tuple(after)

            zero = jnp.zeros((8, SPAN), jnp.float32)
            first = tuple((zero, zero + 1.0, zero, zero, zero) for j in range(GROUPS))
            last = lax.fori_loop(0, BLOCK, depth, first, unroll=True)
            for j in range(GROUPS):
                total, seen, reds, greens, blues = last[j]
                passed = jnp.exp2(total * (-step_size * LOG2E))
                factor = jnp.where(down, 0.5 * passed, -0.5)
                spread = seen - 1.0
                planes = [factor * (spread + color) for color in (reds, greens, blues)]
                planes.append(1.0 - passed)
                for c in range(4):
                    for i in range(SPAN // LANES):
                        rows = pl.ds(j * (SPAN // LANES) + i, 8, stride=TILES)
                        stage_ref[half, c, rows, :] = planes[c][:, i * LANES:(i + 1) * LANES]
        for r in range(relative):
            slot = slot_ref[r]
            rows = pl.ds(pl.multiple_of(lax.rem(slot, 8) * TILES, TILES), TILES)
            for c in range(4):
                outs[r][0, c] = encode(stage_ref[slot // 8, c, rows, :])


def march(counts, order, flip, me, centers, amps, cells, step_size):
    tile_count = counts.shape[0]
    slots = cells.shape[0]
    capacity = slots // tile_count
    scalar = pl.BlockSpec(memory_space=pltpu.SMEM)
    whole = lambda shape: pl.BlockSpec(shape, lambda m: (0,) * len(shape))
    block = pl.BlockSpec((1, 4, TILES, LANES), lambda m: (m, 0, 0, 0))
    return pl.pallas_call(
        functools.partial(march_kernel, step_size, tile_count, tile_count),
        grid=(capacity,),
        in_specs=[scalar] * 4 + [
            whole((1, KNOTS)),
            whole((4, KNOTS)),
            pl.BlockSpec((tile_count, cells.shape[1]), lambda m: (m, 0)),
        ],
        out_specs=[block] * tile_count,
        out_shape=[jax.ShapeDtypeStruct((capacity, 4, TILES, LANES), jnp.int16)] * tile_count,
        scratch_shapes=[
            pltpu.VMEM((KNOTS, 8, LANES), jnp.float32),
            pltpu.VMEM((4 * STACK, 3 * KNOTS * STACK), jnp.bfloat16),
            pltpu.VMEM((tile_count // 8, 4, 8 * TILES, LANES), jnp.float32),
            pltpu.SMEM((tile_count,), jnp.int32),
        ],
        compiler_params=pltpu.CompilerParams(vmem_limit_bytes=MARCH_GRANT),
        name="march",
    )(counts, order, flip, me, centers.reshape(1, KNOTS), amps, cells)


def split_rows(image, kept_ref, given_ref, low, row_share):
    for n in range(kept_ref.shape[1] // row_share):
        mine = pl.multiple_of((2 * n + low) * row_share, row_share)
        theirs = pl.multiple_of((2 * n + 1 - low) * row_share, row_share)
        for c in range(4):
            kept_ref[c, n * row_share:(n + 1) * row_share] = image[c, pl.ds(mine, row_share)]
            given_ref[c, n * row_share:(n + 1) * row_share] = image[c, pl.ds(theirs, row_share)]


def gather_kernel(tile_count, row_share, *refs):
    counts_ref, order_ref, flip_ref, me_ref, layer_ref, home_ref = refs[:6]
    kept_ref, given_ref, brick_ref, image_ref, own_ref, own_sem = refs[5 + tile_count:]
    arrived = (own_ref,) + refs[6:5 + tile_count]
    own_copy = pltpu.make_async_copy(home_ref, own_ref, own_sem)
    own_copy.start()
    me = me_ref[0]
    position = position_of(order_ref, me, tile_count)
    starts = [jnp.int32(0)]
    for i in range(tile_count):
        starts.append(starts[-1] + counts_ref[i])
    for r in [*range(1, tile_count), 0]:
        if r == 0:
            own_copy.wait()
        owner = lax.rem(me - r + tile_count, tile_count)
        start = jnp.int32(0)
        for i in range(tile_count):
            start = jnp.where(owner == i, starts[i], start)
        offset = lax.rem(position - start + tile_count * 64, tile_count)
        level = (start + offset - position) // tile_count
        held = (counts_ref[owner] - offset + tile_count - 1) // tile_count

        def place(m, carry, r=r, level=level):
            brick_ref[level + m] = decode(arrived[r][m])
            return carry

        lax.fori_loop(0, held, place, 0)
    flip = flip_ref[me] == 1
    lane = lax.broadcasted_iota(jnp.int32, (TILES, LANES), 1) // BLOCK
    per_row = LANES // BLOCK
    for by in range(BY):
        images = []
        for bx in range(BX):
            layers = [(bz * BY + by) * BX + bx for bz in range(DB)]
            parts = None
            for n in range(DB):
                index = jnp.where(flip, layers[n], layers[DB - 1 - n])
                new = [brick_ref[index, c] for c in range(4)]
                if parts is None:
                    parts = new
                else:
                    uncovered = 1.0 - new[3]
                    parts = [new[c] + uncovered * parts[c] for c in range(4)]
            images.append(parts)
        for c in range(4):
            for s in range(per_row):
                line = None
                for bx in range(BX):
                    turn = (bx - s) * BLOCK % LANES
                    moved = images[bx][c]
                    if turn:
                        moved = pltpu.roll(moved, turn, 1)
                    line = moved if line is None else jnp.where(lane == bx, moved, line)
                image_ref[c, pl.ds(by * BLOCK + s, TILES, stride=per_row), :] = line
    split_rows(image_ref, kept_ref, given_ref, layer_ref[0] & 1, row_share)


def gather(counts, order, flip, me, layer, arrived, row_share):
    tile_count = counts.shape[0]
    scalar = pl.BlockSpec(memory_space=pltpu.SMEM)
    vmem = pl.BlockSpec(memory_space=pltpu.VMEM)
    rows, width = BY * BLOCK, BX * BLOCK
    half = jax.ShapeDtypeStruct((4, rows // 2, width), jnp.float32)
    return pl.pallas_call(
        functools.partial(gather_kernel, tile_count, row_share),
        in_specs=[scalar] * 5 + [pl.BlockSpec(memory_space=pltpu.HBM)] + [vmem] * (tile_count - 1),
        out_specs=[vmem] * 2,
        out_shape=[half, half],
        scratch_shapes=[
            pltpu.VMEM((DB * BY * BX, 4, TILES, LANES), jnp.float32),
            pltpu.VMEM((4, rows, width), jnp.float32),
            pltpu.VMEM(arrived[0].shape, arrived[0].dtype),
            pltpu.SemaphoreType.DMA,
        ],
        compiler_params=pltpu.CompilerParams(vmem_limit_bytes=GRANT),
        name="gather",
    )(counts, order, flip, me, layer, *arrived)


def blend_kernel(bit, row_share, *refs):
    flip_ref, me_ref, layer_ref, kept_ref, other_ref = refs[:5]
    side = layer_ref[0] >> bit & 1
    front = side == flip_ref[me_ref[0]]
    last = len(refs) == 6
    out_ref = refs[-1]

    def blend(near_ref, far_ref):
        uncovered = 1.0 - near_ref[3]
        for c in range(4):
            out_ref[c] = near_ref[c] + uncovered * far_ref[c]

    @pl.when(front)
    def _():
        blend(kept_ref, other_ref)

    @pl.when(jnp.logical_not(front))
    def _():
        blend(other_ref, kept_ref)

    if not last:
        split_rows(out_ref, refs[5], refs[6], layer_ref[0] >> (bit + 1) & 1, row_share)


def blend(flip, me, layer, kept, other, bit, row_share):
    scalar = pl.BlockSpec(memory_space=pltpu.SMEM)
    vmem = pl.BlockSpec(memory_space=pltpu.VMEM)
    last = kept.shape[1] == row_share
    whole = jax.ShapeDtypeStruct(kept.shape, jnp.float32)
    half = jax.ShapeDtypeStruct((4, kept.shape[1] // 2, kept.shape[2]), jnp.float32)
    return pl.pallas_call(
        functools.partial(blend_kernel, bit, row_share),
        in_specs=[scalar] * 3 + [vmem] * 2,
        out_specs=vmem if last else [vmem] * 2,
        out_shape=whole if last else [half, half],
        scratch_shapes=[] if last else [pltpu.VMEM(kept.shape, jnp.float32)],
        compiler_params=pltpu.CompilerParams(vmem_limit_bytes=GRANT),
        name="blend",
    )(flip, me, layer, kept, other)


def swapped(block, axis, bit):
    count = lax.axis_size(axis)
    return lax.ppermute(block, axis, [(i, i ^ 1 << bit) for i in range(count)])


def body(owned_blocks, slot_counts, brick_order, view_flip, tf_centers, tf_amps):
    tile_count = lax.axis_size("tile")
    depth_count = lax.axis_size("depth")
    step_size = 1.5 / (depth_count * DB * BLOCK)
    me = lax.axis_index("tile").astype(jnp.int32).reshape(1)
    layer = lax.axis_index("depth").astype(jnp.int32).reshape(1)
    counts, order = slot_counts[0], brick_order[0]
    sent = march(counts, order, view_flip, me, tf_centers, tf_amps, owned_blocks[0], step_size)
    arrived = [sent[0]]
    for r in range(1, tile_count):
        route = [(i, (i + r) % tile_count) for i in range(tile_count)]
        arrived.append(lax.ppermute(sent[r], "tile", route))
    row_share = BY * BLOCK // depth_count
    kept, given = gather(counts, order, view_flip, me, layer, arrived, row_share)
    levels = depth_count.bit_length() - 1
    for bit in range(levels):
        other = swapped(given, "depth", bit)
        blended = blend(view_flip, me, layer, kept, other, bit, row_share)
        if bit < levels - 1:
            kept, given = blended
    return blended


def solution(mesh):
    in_specs = (P("depth", "tile", None), P("depth", None), P("depth", None), P(), P(), P())
    out_specs = P(None, "depth", "tile")
    return jax.shard_map(body, mesh=mesh, in_specs=in_specs, out_specs=out_specs, check_vma=False)
```

```python
import functools
import math

import jax
import jax.numpy as jnp
from jax import lax
from jax.experimental import pallas as pl
from jax.experimental.pallas import tpu as pltpu
from jax.sharding import PartitionSpec as P

BLOCK = 32
BX = 4
BY = 4
DB = 2
KNOTS = 8
PIXELS = BLOCK * BLOCK
LANES = 128
TILES = PIXELS // LANES
BUMP_SCALE = 4.0
LOG2E = math.log2(math.e)
ROOT = math.sqrt(BUMP_SCALE * LOG2E)
CODE_TOP = 65535.0
CODE_MID = 32767.5
GRANT = 12 << 20
MARCH_GRANT = 61 << 20
SPAN = 1024
GROUPS = PIXELS // SPAN
STACK = 8 * GROUPS
PACK = 16 // 8


def exclusive_start(counts_ref, index, tile_count):
    start = jnp.int32(0)
    for i in range(tile_count):
        start = start + jnp.where(i < index, counts_ref[i], 0)
    return start


def position_of(order_ref, tile, tile_count):
    position = jnp.int32(0)
    for i in range(tile_count):
        position = position + jnp.where(order_ref[i] == tile, i, 0)
    return position


def encode(image):
    root = jnp.exp2(jnp.log(jnp.maximum(image, 0.0)) * (0.25 * LOG2E))
    code = jnp.round(jnp.minimum(root, 1.0) * CODE_TOP - CODE_MID)
    return code.astype(jnp.int32).astype(jnp.int16)


def decode(code):
    root = (code.astype(jnp.int32).astype(jnp.float32) + CODE_MID) * (1.0 / CODE_TOP)
    square = root * root
    return square * square


def march_kernel(step_size, tile_count, relative, *refs):
    counts_ref, order_ref, flip_ref, me_ref, center_ref, amp_ref, cells_ref = refs[:7]
    outs = refs[7:7 + relative]
    coef_ref, mix_ref, stage_ref, slot_ref = refs[7 + relative:]
    step = pl.program_id(0)
    me = me_ref[0]
    start = exclusive_start(counts_ref, me, tile_count)
    live = counts_ref[me]

    @pl.when(step == 0)
    def _():
        for r in range(relative):
            tile = lax.rem(me + r, tile_count)
            slot_ref[r] = lax.rem(
                position_of(order_ref, tile, tile_count) - start + tile_count * 64, tile_count
            )
        w = center_ref[...] * ROOT
        folded = amp_ref[...] * jnp.exp2(-w * w)
        channel = lax.broadcasted_iota(jnp.int32, (4, 1), 0)
        folded = folded * jnp.where(channel == 3, LOG2E, 0.5)
        for k in range(KNOTS):
            coef_ref[k] = jnp.broadcast_to(2.0 * w[:, k:k + 1], (8, LANES))
        knot = lax.broadcasted_iota(jnp.int32, (4, KNOTS * STACK), 1) // STACK
        spread = jnp.zeros((4, KNOTS * STACK), jnp.float32)
        for k in range(KNOTS):
            spread = jnp.where(knot == k, folded[:, k:k + 1], spread)
        coarse = spread.astype(jnp.bfloat16)
        fine = (spread - coarse.astype(jnp.float32)).astype(jnp.bfloat16)
        own = lax.broadcasted_iota(jnp.int32, (STACK, KNOTS * STACK), 0) == lax.rem(
            lax.broadcasted_iota(jnp.int32, (STACK, KNOTS * STACK), 1), STACK
        )
        width = KNOTS * STACK
        for part, amps in enumerate((coarse, fine)):
            amps = amps.astype(jnp.float32)
            for c in range(4):
                first = (part * 4 + c) * STACK
                line = jnp.where(own, amps[c:c + 1], 0.0).astype(jnp.bfloat16)
                mix_ref[first:first + STACK, :width] = line
                mix_ref[first:first + STACK, width:] = line

    @pl.when(step * tile_count < live)
    def _():
        row = lax.broadcasted_iota(jnp.int32, (8, SPAN), 0)
        for half in range(tile_count // 8):
            flip = jnp.zeros((8, SPAN), jnp.int32)
            for s in range(8):
                tile = order_ref[lax.rem(start + half * 8 + s, tile_count)]
                flip = jnp.where(row == s, flip_ref[tile], flip)
            down = flip == 1
            signed_step = jnp.where(down, step_size * LOG2E, -step_size * LOG2E)

            def depth(z, state, half=half, signed_step=signed_step):
                values = []
                for j in range(GROUPS):
                    lane = pl.multiple_of(z * PIXELS + j * SPAN, LANES)
                    raw = cells_ref[half * 8:half * 8 + 8, pl.ds(lane, SPAN)]
                    values.append(raw.astype(jnp.float32) * ROOT)
                bumps = []
                for k in range(KNOTS):
                    center = jnp.concatenate([coef_ref[k]] * (SPAN // LANES), axis=1)
                    bumps += [jnp.exp2(v * (center - v)) for v in values]
                high, low = [], []
                for n in range(0, len(bumps), PACK):
                    bump = jnp.concatenate(bumps[n:n + PACK], axis=0)
                    coarse = bump.astype(jnp.bfloat16)
                    high.append(coarse)
                    low.append((bump - coarse.astype(jnp.float32)).astype(jnp.bfloat16))
                stacked = jnp.concatenate(high + low, axis=0)
                both = jnp.dot(mix_ref[...], stacked, preferred_element_type=jnp.float32)
                fields = both[:4 * STACK] + both[4 * STACK:]
                after = []
                for j in range(GROUPS):
                    red, green, blue, dense = (
                        fields[c * STACK + j * 8:c * STACK + j * 8 + 8] for c in range(4)
                    )
                    total, seen, reds, greens, blues = state[j]
                    total = total + jnp.log(1.0 + jnp.exp2(dense))
                    now = jnp.exp2(signed_step * total)
                    weight = now - seen
                    after.append((
                        total,
                        now,
                        reds + weight * jnp.tanh(red),
                        greens + weight * jnp.tanh(green),
                        blues + weight * jnp.tanh(blue),
                    ))
                return tuple(after)

            zero = jnp.zeros((8, SPAN), jnp.float32)
            first = tuple((zero, zero + 1.0, zero, zero, zero) for j in range(GROUPS))
            last = lax.fori_loop(0, BLOCK, depth, first, unroll=True)
            for j in range(GROUPS):
                total, seen, reds, greens, blues = last[j]
                passed = jnp.exp2(total * (-step_size * LOG2E))
                factor = jnp.where(down, 0.5 * passed, -0.5)
                spread = seen - 1.0
                planes = [factor * (spread + color) for color in (reds, greens, blues)]
                planes.append(1.0 - passed)
                for c in range(4):
                    for i in range(SPAN // LANES):
                        rows = pl.ds(j * (SPAN // LANES) + i, 8, stride=TILES)
                        stage_ref[half, c, rows, :] = planes[c][:, i * LANES:(i + 1) * LANES]
        for r in range(relative):
            slot = slot_ref[r]
            rows = pl.ds(pl.multiple_of(lax.rem(slot, 8) * TILES, TILES), TILES)
            for c in range(4):
                outs[r][0, c] = encode(stage_ref[slot // 8, c, rows, :])


def march(counts, order, flip, me, centers, amps, cells, step_size):
    tile_count = counts.shape[0]
    slots = cells.shape[0]
    capacity = slots // tile_count
    scalar = pl.BlockSpec(memory_space=pltpu.SMEM)
    whole = lambda shape: pl.BlockSpec(shape, lambda m: (0,) * len(shape))
    block = pl.BlockSpec((1, 4, TILES, LANES), lambda m: (m, 0, 0, 0))
    return pl.pallas_call(
        functools.partial(march_kernel, step_size, tile_count, tile_count),
        grid=(capacity,),
        in_specs=[scalar] * 4 + [
            whole((1, KNOTS)),
            whole((4, KNOTS)),
            pl.BlockSpec((tile_count, cells.shape[1]), lambda m: (m, 0)),
        ],
        out_specs=[block] * tile_count,
        out_shape=[jax.ShapeDtypeStruct((capacity, 4, TILES, LANES), jnp.int16)] * tile_count,
        scratch_shapes=[
            pltpu.VMEM((KNOTS, 8, LANES), jnp.float32),
            pltpu.VMEM((8 * STACK, 2 * KNOTS * STACK), jnp.bfloat16),
            pltpu.VMEM((tile_count // 8, 4, 8 * TILES, LANES), jnp.float32),
            pltpu.SMEM((tile_count,), jnp.int32),
        ],
        compiler_params=pltpu.CompilerParams(vmem_limit_bytes=MARCH_GRANT),
        name="march",
    )(counts, order, flip, me, centers.reshape(1, KNOTS), amps, cells)


def split_rows(image, kept_ref, given_ref, low, row_share):
    for n in range(kept_ref.shape[1] // row_share):
        mine = pl.multiple_of((2 * n + low) * row_share, row_share)
        theirs = pl.multiple_of((2 * n + 1 - low) * row_share, row_share)
        for c in range(4):
            kept_ref[c, n * row_share:(n + 1) * row_share] = image[c, pl.ds(mine, row_share)]
            given_ref[c, n * row_share:(n + 1) * row_share] = encode(image[c, pl.ds(theirs, row_share)])


def gather_kernel(tile_count, row_share, last_bit, *refs):
    counts_ref, order_ref, flip_ref, me_ref, layer_ref, home_ref = refs[:6]
    kept_ref, given_ref, front_ref, brick_ref, image_ref, own_ref, own_sem = refs[5 + tile_count:]
    arrived = (own_ref,) + refs[6:5 + tile_count]
    own_copy = pltpu.make_async_copy(home_ref, own_ref, own_sem)
    own_copy.start()
    me = me_ref[0]
    position = position_of(order_ref, me, tile_count)
    starts = [jnp.int32(0)]
    for i in range(tile_count):
        starts.append(starts[-1] + counts_ref[i])
    for r in [*range(1, tile_count), 0]:
        if r == 0:
            own_copy.wait()
        owner = lax.rem(me - r + tile_count, tile_count)
        start = jnp.int32(0)
        for i in range(tile_count):
            start = jnp.where(owner == i, starts[i], start)
        offset = lax.rem(position - start + tile_count * 64, tile_count)
        level = (start + offset - position) // tile_count
        held = (counts_ref[owner] - offset + tile_count - 1) // tile_count

        def place(m, carry, r=r, level=level):
            brick_ref[level + m] = decode(arrived[r][m])
            return carry

        lax.fori_loop(0, held, place, 0)
    flip = flip_ref[me] == 1
    lane = lax.broadcasted_iota(jnp.int32, (TILES, LANES), 1) // BLOCK
    per_row = LANES // BLOCK
    for by in range(BY):
        images = []
        for bx in range(BX):
            layers = [(bz * BY + by) * BX + bx for bz in range(DB)]
            parts = None
            for n in range(DB):
                index = jnp.where(flip, layers[n], layers[DB - 1 - n])
                new = [brick_ref[index, c] for c in range(4)]
                if parts is None:
                    parts = new
                else:
                    uncovered = 1.0 - new[3]
                    parts = [new[c] + uncovered * parts[c] for c in range(4)]
            images.append(parts)
        for c in range(4):
            for s in range(per_row):
                line = None
                for bx in range(BX):
                    turn = (bx - s) * BLOCK % LANES
                    moved = images[bx][c]
                    if turn:
                        moved = pltpu.roll(moved, turn, 1)
                    line = moved if line is None else jnp.where(lane == bx, moved, line)
                image_ref[c, pl.ds(by * BLOCK + s, TILES, stride=per_row), :] = line
    split_rows(image_ref, kept_ref, given_ref, layer_ref[0] & 1, row_share)
    front = (layer_ref[0] >> last_bit & 1) == flip_ref[me]
    front_ref[...] = jnp.broadcast_to(jnp.where(front, 1.0, 0.0), (8, LANES))


def gather(counts, order, flip, me, layer, arrived, row_share, last_bit):
    tile_count = counts.shape[0]
    scalar = pl.BlockSpec(memory_space=pltpu.SMEM)
    vmem = pl.BlockSpec(memory_space=pltpu.VMEM)
    rows, width = BY * BLOCK, BX * BLOCK
    half = jax.ShapeDtypeStruct((4, rows // 2, width), jnp.float32)
    return pl.pallas_call(
        functools.partial(gather_kernel, tile_count, row_share, last_bit),
        in_specs=[scalar] * 5 + [pl.BlockSpec(memory_space=pltpu.HBM)] + [vmem] * (tile_count - 1),
        out_specs=[vmem] * 3,
        out_shape=[
            half,
            jax.ShapeDtypeStruct(half.shape, jnp.int16),
            jax.ShapeDtypeStruct((8, LANES), jnp.float32),
        ],
        scratch_shapes=[
            pltpu.VMEM((DB * BY * BX, 4, TILES, LANES), jnp.float32),
            pltpu.VMEM((4, rows, width), jnp.float32),
            pltpu.VMEM(arrived[0].shape, arrived[0].dtype),
            pltpu.SemaphoreType.DMA,
        ],
        compiler_params=pltpu.CompilerParams(vmem_limit_bytes=GRANT),
        name="gather",
    )(counts, order, flip, me, layer, pltpu.with_memory_space_constraint(arrived[0], pltpu.HBM), *arrived[1:])


def blend_kernel(bit, row_share, *refs):
    flip_ref, me_ref, layer_ref, kept_ref, other_ref, kept_out, given_out, image_ref = refs
    front = (layer_ref[0] >> bit & 1) == flip_ref[me_ref[0]]
    kept_open = 1.0 - kept_ref[3]
    other_open = 1.0 - decode(other_ref[3])
    kept_part = jnp.where(front, 1.0, other_open)
    other_part = jnp.where(front, kept_open, 1.0)
    for c in range(4):
        image_ref[c] = kept_part * kept_ref[c] + other_part * decode(other_ref[c])
    split_rows(image_ref, kept_out, given_out, layer_ref[0] >> (bit + 1) & 1, row_share)


def blend(flip, me, layer, kept, other, bit, row_share):
    scalar = pl.BlockSpec(memory_space=pltpu.SMEM)
    vmem = pl.BlockSpec(memory_space=pltpu.VMEM)
    half = (4, kept.shape[1] // 2, kept.shape[2])
    return pl.pallas_call(
        functools.partial(blend_kernel, bit, row_share),
        in_specs=[scalar] * 3 + [vmem] * 2,
        out_specs=[vmem] * 2,
        out_shape=[
            jax.ShapeDtypeStruct(half, jnp.float32),
            jax.ShapeDtypeStruct(half, jnp.int16),
        ],
        scratch_shapes=[pltpu.VMEM(kept.shape, jnp.float32)],
        compiler_params=pltpu.CompilerParams(vmem_limit_bytes=GRANT),
        name="blend",
    )(flip, me, layer, kept, other)


def last_blend(front, kept, coded):
    other = decode(coded)
    front = front[:1][None] > 0.5
    kept_part = jnp.where(front, 1.0, 1.0 - other[3:])
    other_part = jnp.where(front, 1.0 - kept[3:], 1.0)
    return kept_part * kept + other_part * other


def swapped(block, axis, bit):
    count = lax.axis_size(axis)
    return lax.ppermute(block, axis, [(i, i ^ 1 << bit) for i in range(count)])


def body(owned_blocks, slot_counts, brick_order, view_flip, tf_centers, tf_amps):
    tile_count = lax.axis_size("tile")
    depth_count = lax.axis_size("depth")
    step_size = 1.5 / (depth_count * DB * BLOCK)
    me = lax.axis_index("tile").astype(jnp.int32).reshape(1)
    layer = lax.axis_index("depth").astype(jnp.int32).reshape(1)
    counts, order = slot_counts[0], brick_order[0]
    sent = march(counts, order, view_flip, me, tf_centers, tf_amps, owned_blocks[0], step_size)
    arrived = [sent[0]]
    for r in range(1, tile_count):
        route = [(i, (i + r) % tile_count) for i in range(tile_count)]
        arrived.append(lax.ppermute(sent[r], "tile", route))
    row_share = BY * BLOCK // depth_count
    levels = depth_count.bit_length() - 1
    kept, given, front = gather(
        counts, order, view_flip, me, layer, arrived, row_share, levels - 1
    )
    for bit in range(levels - 1):
        other = swapped(given, "depth", bit)
        kept, given = blend(view_flip, me, layer, kept, other, bit, row_share)
    return last_blend(front, kept, swapped(given, "depth", levels - 1))


def solution(mesh):
    in_specs = (P("depth", "tile", None), P("depth", None), P("depth", None), P(), P(), P())
    out_specs = P(None, "depth", "tile")
    return jax.shard_map(body, mesh=mesh, in_specs=in_specs, out_specs=out_specs, check_vma=False)
```

```python
import functools
import math

import jax
import jax.numpy as jnp
from jax import lax
from jax.experimental import pallas as pl
from jax.experimental.pallas import tpu as pltpu
from jax.sharding import PartitionSpec as P

BLOCK = 32
BX = 4
BY = 4
DB = 2
KNOTS = 8
PIXELS = BLOCK * BLOCK
LANES = 128
TILES = PIXELS // LANES
BUMP_SCALE = 4.0
LOG2E = math.log2(math.e)
ROOT = math.sqrt(BUMP_SCALE * LOG2E)
CODE_TOP = 65535.0
CODE_MID = 32767.5
GRANT = 12 << 20
MARCH_GRANT = 61 << 20
SPAN = 512
GROUPS = PIXELS // SPAN
STACK = 8 * GROUPS
PACK = 16 // 8


def exclusive_start(counts_ref, index, tile_count):
    start = jnp.int32(0)
    for i in range(tile_count):
        start = start + jnp.where(i < index, counts_ref[i], 0)
    return start


def position_of(order_ref, tile, tile_count):
    position = jnp.int32(0)
    for i in range(tile_count):
        position = position + jnp.where(order_ref[i] == tile, i, 0)
    return position


def encode(image):
    root = jnp.exp2(jnp.log(jnp.maximum(image, 0.0)) * (0.25 * LOG2E))
    code = jnp.round(jnp.minimum(root, 1.0) * CODE_TOP - CODE_MID)
    return code.astype(jnp.int32).astype(jnp.int16)


def decode(code):
    root = (code.astype(jnp.int32).astype(jnp.float32) + CODE_MID) * (1.0 / CODE_TOP)
    square = root * root
    return square * square


def march_kernel(step_size, tile_count, relative, *refs):
    counts_ref, order_ref, flip_ref, me_ref, center_ref, amp_ref, cells_ref = refs[:7]
    outs = refs[7:7 + relative]
    coef_ref, mix_ref, stage_ref, slot_ref = refs[7 + relative:]
    step = pl.program_id(0)
    me = me_ref[0]
    start = exclusive_start(counts_ref, me, tile_count)
    live = counts_ref[me]

    @pl.when(step == 0)
    def _():
        for r in range(relative):
            tile = lax.rem(me + r, tile_count)
            slot_ref[r] = lax.rem(
                position_of(order_ref, tile, tile_count) - start + tile_count * 64, tile_count
            )
        w = center_ref[...] * ROOT
        folded = amp_ref[...] * jnp.exp2(-w * w)
        channel = lax.broadcasted_iota(jnp.int32, (4, 1), 0)
        folded = folded * jnp.where(channel == 3, LOG2E, 0.5)
        for k in range(KNOTS):
            coef_ref[k] = jnp.broadcast_to(2.0 * w[:, k:k + 1], (8, LANES))
        knot = lax.broadcasted_iota(jnp.int32, (4, KNOTS * STACK), 1) // STACK
        spread = jnp.zeros((4, KNOTS * STACK), jnp.float32)
        for k in range(KNOTS):
            spread = jnp.where(knot == k, folded[:, k:k + 1], spread)
        coarse = spread.astype(jnp.bfloat16)
        fine = (spread - coarse.astype(jnp.float32)).astype(jnp.bfloat16)
        own = lax.broadcasted_iota(jnp.int32, (STACK, KNOTS * STACK), 0) == lax.rem(
            lax.broadcasted_iota(jnp.int32, (STACK, KNOTS * STACK), 1), STACK
        )
        width = KNOTS * STACK
        for part, amps in enumerate((coarse, fine)):
            amps = amps.astype(jnp.float32)
            for c in range(4):
                first = (part * 4 + c) * STACK
                line = jnp.where(own, amps[c:c + 1], 0.0).astype(jnp.bfloat16)
                mix_ref[first:first + STACK, :width] = line
                mix_ref[first:first + STACK, width:] = line

    @pl.when(step * tile_count < live)
    def _():
        row = lax.broadcasted_iota(jnp.int32, (8, SPAN), 0)
        for half in range(tile_count // 8):
            flip = jnp.zeros((8, SPAN), jnp.int32)
            for s in range(8):
                tile = order_ref[lax.rem(start + half * 8 + s, tile_count)]
                flip = jnp.where(row == s, flip_ref[tile], flip)
            down = flip == 1
            signed_step = jnp.where(down, step_size, -step_size)

            def depth(z, state, half=half, signed_step=signed_step):
                values = []
                for j in range(GROUPS):
                    lane = pl.multiple_of(z * PIXELS + j * SPAN, LANES)
                    raw = cells_ref[half * 8:half * 8 + 8, pl.ds(lane, SPAN)]
                    values.append(raw.astype(jnp.float32) * ROOT)
                bumps = []
                for k in range(KNOTS):
                    center = jnp.concatenate([coef_ref[k]] * (SPAN // LANES), axis=1)
                    bumps += [jnp.exp2(v * (center - v)) for v in values]
                high, low = [], []
                for n in range(0, len(bumps), PACK):
                    bump = jnp.concatenate(bumps[n:n + PACK], axis=0)
                    coarse = bump.astype(jnp.bfloat16)
                    high.append(coarse)
                    low.append((bump - coarse.astype(jnp.float32)).astype(jnp.bfloat16))
                stacked = jnp.concatenate(high + low, axis=0)
                both = jnp.dot(mix_ref[...], stacked, preferred_element_type=jnp.float32)
                fields = both[:4 * STACK] + both[4 * STACK:]
                after = []
                for j in range(GROUPS):
                    red, green, blue, dense = (
                        fields[c * STACK + j * 8:c * STACK + j * 8 + 8] for c in range(4)
                    )
                    total, seen, reds, greens, blues = state[j]
                    total = total + lax.log2(1.0 + jnp.exp2(dense))
                    now = jnp.exp2(signed_step * total)
                    weight = now - seen
                    after.append((
                        total,
                        now,
                        reds + weight * jnp.tanh(red),
                        greens + weight * jnp.tanh(green),
                        blues + weight * jnp.tanh(blue),
                    ))
                return tuple(after)

            zero = jnp.zeros((8, SPAN), jnp.float32)
            first = tuple((zero, zero + 1.0, zero, zero, zero) for j in range(GROUPS))
            last = lax.fori_loop(0, BLOCK, depth, first, unroll=True)
            for j in range(GROUPS):
                total, seen, reds, greens, blues = last[j]
                passed = jnp.exp2(total * -step_size)
                factor = jnp.where(down, 0.5 * passed, -0.5)
                spread = seen - 1.0
                planes = [factor * (spread + color) for color in (reds, greens, blues)]
                planes.append(1.0 - passed)
                for c in range(4):
                    for i in range(SPAN // LANES):
                        rows = pl.ds(j * (SPAN // LANES) + i, 8, stride=TILES)
                        stage_ref[half, c, rows, :] = planes[c][:, i * LANES:(i + 1) * LANES]
        for r in range(relative):
            slot = slot_ref[r]
            rows = pl.ds(pl.multiple_of(lax.rem(slot, 8) * TILES, TILES), TILES)
            for c in range(4):
                outs[r][0, c] = encode(stage_ref[slot // 8, c, rows, :])


def march(counts, order, flip, me, centers, amps, cells, step_size):
    tile_count = counts.shape[0]
    slots = cells.shape[0]
    capacity = slots // tile_count
    scalar = pl.BlockSpec(memory_space=pltpu.SMEM)
    whole = lambda shape: pl.BlockSpec(shape, lambda m: (0,) * len(shape))
    block = pl.BlockSpec((1, 4, TILES, LANES), lambda m: (m, 0, 0, 0))
    return pl.pallas_call(
        functools.partial(march_kernel, step_size, tile_count, tile_count),
        grid=(capacity,),
        in_specs=[scalar] * 4 + [
            whole((1, KNOTS)),
            whole((4, KNOTS)),
            pl.BlockSpec((tile_count, cells.shape[1]), lambda m: (m, 0)),
        ],
        out_specs=[block] * tile_count,
        out_shape=[jax.ShapeDtypeStruct((capacity, 4, TILES, LANES), jnp.int16)] * tile_count,
        scratch_shapes=[
            pltpu.VMEM((KNOTS, 8, LANES), jnp.float32),
            pltpu.VMEM((8 * STACK, 2 * KNOTS * STACK), jnp.bfloat16),
            pltpu.VMEM((tile_count // 8, 4, 8 * TILES, LANES), jnp.float32),
            pltpu.SMEM((tile_count,), jnp.int32),
        ],
        compiler_params=pltpu.CompilerParams(vmem_limit_bytes=MARCH_GRANT),
        name="march",
    )(counts, order, flip, me, centers.reshape(1, KNOTS), amps, cells)


def split_rows(image, kept_ref, given_ref, low, row_share):
    for n in range(kept_ref.shape[1] // row_share):
        mine = pl.multiple_of((2 * n + low) * row_share, row_share)
        theirs = pl.multiple_of((2 * n + 1 - low) * row_share, row_share)
        for c in range(4):
            kept_ref[c, n * row_share:(n + 1) * row_share] = image[c, pl.ds(mine, row_share)]
            given_ref[c, n * row_share:(n + 1) * row_share] = encode(image[c, pl.ds(theirs, row_share)])


def place_images(counts_ref, order_ref, me, brick_ref, arrived, tile_count):
    position = position_of(order_ref, me, tile_count)
    starts = [jnp.int32(0)]
    for i in range(tile_count):
        starts.append(starts[-1] + counts_ref[i])
    for r, wait, images_ref in arrived:
        wait()
        owner = lax.rem(me - r + tile_count, tile_count)
        start = jnp.int32(0)
        for i in range(tile_count):
            start = jnp.where(owner == i, starts[i], start)
        offset = lax.rem(position - start + tile_count * 64, tile_count)
        level = (start + offset - position) // tile_count
        held = (counts_ref[owner] - offset + tile_count - 1) // tile_count

        def place(m, carry, images_ref=images_ref, level=level):
            brick_ref[level + m] = decode(images_ref[m])
            return carry

        lax.fori_loop(0, held, place, 0)


def ready():
    pass


def place_kernel(tile_count, *refs):
    counts_ref, order_ref, me_ref, home_ref = refs[:4]
    brick_ref, own_ref, own_sem = refs[-3:]
    own_copy = pltpu.make_async_copy(home_ref, own_ref, own_sem)
    own_copy.start()
    arrived = [(r + 1, ready, ref) for r, ref in enumerate(refs[4:-3])]
    arrived.append((0, own_copy.wait, own_ref))
    place_images(counts_ref, order_ref, me_ref[0], brick_ref, arrived, tile_count)


def place_early(counts, order, me, arrived):
    tile_count = counts.shape[0]
    scalar = pl.BlockSpec(memory_space=pltpu.SMEM)
    vmem = pl.BlockSpec(memory_space=pltpu.VMEM)
    home = pltpu.with_memory_space_constraint(arrived[0], pltpu.HBM)
    brick = (DB * BY * BX, 4, TILES, LANES)
    return pl.pallas_call(
        functools.partial(place_kernel, tile_count),
        in_specs=[scalar] * 3 + [pl.BlockSpec(memory_space=pltpu.HBM)] + [vmem] * (len(arrived) - 1),
        out_specs=vmem,
        out_shape=jax.ShapeDtypeStruct(brick, jnp.float32),
        scratch_shapes=[
            pltpu.VMEM(home.shape, home.dtype),
            pltpu.SemaphoreType.DMA,
        ],
        compiler_params=pltpu.CompilerParams(vmem_limit_bytes=GRANT),
        cost_estimate=pl.CostEstimate(flops=1 << 20, bytes_accessed=1 << 20, transcendentals=0),
        name="place",
    )(counts, order, me, home, *arrived[1:])


def gather_kernel(tile_count, row_share, last_bit, *refs):
    counts_ref, order_ref, flip_ref, me_ref, layer_ref, early_ref = refs[:6]
    kept_ref, given_ref, front_ref, brick_ref, image_ref = refs[-5:]
    late = refs[6:-5]
    me = me_ref[0]
    brick_ref[...] = early_ref[...]
    arrived = [(tile_count - len(late) + n, ready, ref) for n, ref in enumerate(late)]
    place_images(counts_ref, order_ref, me, brick_ref, arrived, tile_count)
    flip = flip_ref[me] == 1
    lane = lax.broadcasted_iota(jnp.int32, (TILES, LANES), 1) // BLOCK
    per_row = LANES // BLOCK
    for by in range(BY):
        images = []
        for bx in range(BX):
            layers = [(bz * BY + by) * BX + bx for bz in range(DB)]
            parts = None
            for n in range(DB):
                index = jnp.where(flip, layers[n], layers[DB - 1 - n])
                new = [brick_ref[index, c] for c in range(4)]
                if parts is None:
                    parts = new
                else:
                    uncovered = 1.0 - new[3]
                    parts = [new[c] + uncovered * parts[c] for c in range(4)]
            images.append(parts)
        for c in range(4):
            for s in range(per_row):
                line = None
                for bx in range(BX):
                    turn = (bx - s) * BLOCK % LANES
                    moved = images[bx][c]
                    if turn:
                        moved = pltpu.roll(moved, turn, 1)
                    line = moved if line is None else jnp.where(lane == bx, moved, line)
                image_ref[c, pl.ds(by * BLOCK + s, TILES, stride=per_row), :] = line
    split_rows(image_ref, kept_ref, given_ref, layer_ref[0] & 1, row_share)
    front = (layer_ref[0] >> last_bit & 1) == flip_ref[me]
    front_ref[...] = jnp.broadcast_to(jnp.where(front, 1.0, 0.0), (8, LANES))


def gather(counts, order, flip, me, layer, early, late, row_share, last_bit):
    tile_count = counts.shape[0]
    scalar = pl.BlockSpec(memory_space=pltpu.SMEM)
    vmem = pl.BlockSpec(memory_space=pltpu.VMEM)
    rows, width = BY * BLOCK, BX * BLOCK
    half = (4, rows // 2, width)
    return pl.pallas_call(
        functools.partial(gather_kernel, tile_count, row_share, last_bit),
        in_specs=[scalar] * 5 + [vmem] * (1 + len(late)),
        out_specs=[vmem] * 3,
        out_shape=[
            jax.ShapeDtypeStruct(half, jnp.float32),
            jax.ShapeDtypeStruct(half, jnp.int16),
            jax.ShapeDtypeStruct((8, LANES), jnp.float32),
        ],
        scratch_shapes=[
            pltpu.VMEM(early.shape, jnp.float32),
            pltpu.VMEM((4, rows, width), jnp.float32),
        ],
        compiler_params=pltpu.CompilerParams(vmem_limit_bytes=GRANT),
        name="gather",
    )(counts, order, flip, me, layer, early, *late)


def blend_kernel(bit, row_share, *refs):
    flip_ref, me_ref, layer_ref, kept_ref, other_ref, kept_out, given_out, image_ref = refs
    front = (layer_ref[0] >> bit & 1) == flip_ref[me_ref[0]]
    kept_open = 1.0 - kept_ref[3]
    other_open = 1.0 - decode(other_ref[3])
    kept_part = jnp.where(front, 1.0, other_open)
    other_part = jnp.where(front, kept_open, 1.0)
    for c in range(4):
        image_ref[c] = kept_part * kept_ref[c] + other_part * decode(other_ref[c])
    split_rows(image_ref, kept_out, given_out, layer_ref[0] >> (bit + 1) & 1, row_share)


def blend(flip, me, layer, kept, other, bit, row_share):
    scalar = pl.BlockSpec(memory_space=pltpu.SMEM)
    vmem = pl.BlockSpec(memory_space=pltpu.VMEM)
    half = (4, kept.shape[1] // 2, kept.shape[2])
    return pl.pallas_call(
        functools.partial(blend_kernel, bit, row_share),
        in_specs=[scalar] * 3 + [vmem] * 2,
        out_specs=[vmem] * 2,
        out_shape=[
            jax.ShapeDtypeStruct(half, jnp.float32),
            jax.ShapeDtypeStruct(half, jnp.int16),
        ],
        scratch_shapes=[pltpu.VMEM(kept.shape, jnp.float32)],
        compiler_params=pltpu.CompilerParams(vmem_limit_bytes=GRANT),
        name="blend",
    )(flip, me, layer, kept, other)


def last_blend(front, kept, coded):
    other = decode(coded)
    front = front[:1][None] > 0.5
    kept_part = jnp.where(front, 1.0, 1.0 - other[3:])
    other_part = jnp.where(front, 1.0 - kept[3:], 1.0)
    return kept_part * kept + other_part * other


def swapped(block, axis, bit):
    count = lax.axis_size(axis)
    return lax.ppermute(block, axis, [(i, i ^ 1 << bit) for i in range(count)])


def body(owned_blocks, slot_counts, brick_order, view_flip, tf_centers, tf_amps):
    tile_count = lax.axis_size("tile")
    depth_count = lax.axis_size("depth")
    step_size = 1.5 / (depth_count * DB * BLOCK)
    me = lax.axis_index("tile").astype(jnp.int32).reshape(1)
    layer = lax.axis_index("depth").astype(jnp.int32).reshape(1)
    counts, order = slot_counts[0], brick_order[0]
    sent = march(counts, order, view_flip, me, tf_centers, tf_amps, owned_blocks[0], step_size)
    arrived = [sent[0]]
    for r in range(1, tile_count):
        route = [(i, (i + r) % tile_count) for i in range(tile_count)]
        arrived.append(lax.ppermute(sent[r], "tile", route))
    early = place_early(counts, order, me, arrived[:tile_count // 2])
    row_share = BY * BLOCK // depth_count
    levels = depth_count.bit_length() - 1
    kept, given, front = gather(
        counts, order, view_flip, me, layer, early, arrived[tile_count // 2:], row_share, levels - 1
    )
    for bit in range(levels - 1):
        other = swapped(given, "depth", bit)
        kept, given = blend(view_flip, me, layer, kept, other, bit, row_share)
    return last_blend(front, kept, swapped(given, "depth", levels - 1))


def solution(mesh):
    in_specs = (P("depth", "tile", None), P("depth", None), P("depth", None), P(), P(), P())
    out_specs = P(None, "depth", "tile")
    return jax.shard_map(body, mesh=mesh, in_specs=in_specs, out_specs=out_specs, check_vma=False)
```

```python
import functools
import math

import jax
import jax.numpy as jnp
from jax import lax
from jax.experimental import pallas as pl
from jax.experimental.pallas import tpu as pltpu
from jax.sharding import PartitionSpec as P

BLOCK = 32
BX = 4
BY = 4
DB = 2
KNOTS = 8
PIXELS = BLOCK * BLOCK
LANES = 128
TILES = PIXELS // LANES
BUMP_SCALE = 4.0
LOG2E = math.log2(math.e)
ROOT = math.sqrt(BUMP_SCALE * LOG2E)
CODE_TOP = 65535.0
CODE_MID = 32767.5
GRANT = 12 << 20
SPAN = 512
GROUPS = PIXELS // SPAN
STACK = 8 * GROUPS
PACK = 16 // 8


def exclusive_start(counts_ref, index, tile_count):
    start = jnp.int32(0)
    for i in range(tile_count):
        start = start + jnp.where(i < index, counts_ref[i], 0)
    return start


def position_of(order_ref, tile, tile_count):
    position = jnp.int32(0)
    for i in range(tile_count):
        position = position + jnp.where(order_ref[i] == tile, i, 0)
    return position


def encode(image):
    root = jnp.exp2(jnp.log(jnp.maximum(image, 0.0)) * (0.25 * LOG2E))
    code = jnp.round(jnp.minimum(root, 1.0) * CODE_TOP - CODE_MID)
    return code.astype(jnp.int32).astype(jnp.int16)


def decode(code):
    root = (code.astype(jnp.int32).astype(jnp.float32) + CODE_MID) * (1.0 / CODE_TOP)
    square = root * root
    return square * square


def march_kernel(step_size, tile_count, relative, *refs):
    counts_ref, order_ref, flip_ref, me_ref, center_ref, amp_ref, cells_ref = refs[:7]
    outs = refs[7:7 + relative]
    coef_ref, mix_ref, stage_ref, slot_ref = refs[7 + relative:]
    step = pl.program_id(0)
    me = me_ref[0]
    start = exclusive_start(counts_ref, me, tile_count)
    live = counts_ref[me]

    @pl.when(step == 0)
    def _():
        for r in range(relative):
            tile = lax.rem(me + r, tile_count)
            slot_ref[r] = lax.rem(
                position_of(order_ref, tile, tile_count) - start + tile_count * 64, tile_count
            )
        w = center_ref[...] * ROOT
        folded = amp_ref[...] * jnp.exp2(-w * w)
        channel = lax.broadcasted_iota(jnp.int32, (4, 1), 0)
        folded = folded * jnp.where(channel == 3, LOG2E, 0.5)
        for k in range(KNOTS):
            coef_ref[k] = jnp.broadcast_to(2.0 * w[:, k:k + 1], (8, LANES))
        knot = lax.broadcasted_iota(jnp.int32, (4, KNOTS * STACK), 1) // STACK
        spread = jnp.zeros((4, KNOTS * STACK), jnp.float32)
        for k in range(KNOTS):
            spread = jnp.where(knot == k, folded[:, k:k + 1], spread)
        coarse = spread.astype(jnp.bfloat16)
        fine = (spread - coarse.astype(jnp.float32)).astype(jnp.bfloat16)
        own = lax.broadcasted_iota(jnp.int32, (STACK, KNOTS * STACK), 0) == lax.rem(
            lax.broadcasted_iota(jnp.int32, (STACK, KNOTS * STACK), 1), STACK
        )
        width = KNOTS * STACK
        for part, amps in enumerate((coarse, fine)):
            amps = amps.astype(jnp.float32)
            for c in range(4):
                first = (part * 4 + c) * STACK
                line = jnp.where(own, amps[c:c + 1], 0.0).astype(jnp.bfloat16)
                mix_ref[first:first + STACK, :width] = line
                mix_ref[first:first + STACK, width:] = line

    @pl.when(step * tile_count < live)
    def _():
        row = lax.broadcasted_iota(jnp.int32, (8, SPAN), 0)
        for half in range(tile_count // 8):
            flip = jnp.zeros((8, SPAN), jnp.int32)
            for s in range(8):
                tile = order_ref[lax.rem(start + half * 8 + s, tile_count)]
                flip = jnp.where(row == s, flip_ref[tile], flip)
            down = flip == 1
            signed_step = jnp.where(down, step_size, -step_size)

            def depth(z, state, half=half, signed_step=signed_step):
                values = []
                for j in range(GROUPS):
                    lane = pl.multiple_of(z * PIXELS + j * SPAN, LANES)
                    raw = cells_ref[half * 8:half * 8 + 8, pl.ds(lane, SPAN)]
                    values.append(raw.astype(jnp.float32) * ROOT)
                bumps = []
                for k in range(KNOTS):
                    center = jnp.concatenate([coef_ref[k]] * (SPAN // LANES), axis=1)
                    bumps += [jnp.exp2(v * (center - v)) for v in values]
                high, low = [], []
                for n in range(0, len(bumps), PACK):
                    bump = jnp.concatenate(bumps[n:n + PACK], axis=0)
                    coarse = bump.astype(jnp.bfloat16)
                    high.append(coarse)
                    low.append((bump - coarse.astype(jnp.float32)).astype(jnp.bfloat16))
                stacked = jnp.concatenate(high + low, axis=0)
                both = jnp.dot(mix_ref[...], stacked, preferred_element_type=jnp.float32)
                fields = both[:4 * STACK] + both[4 * STACK:]
                after = []
                for j in range(GROUPS):
                    red, green, blue, dense = (
                        fields[c * STACK + j * 8:c * STACK + j * 8 + 8] for c in range(4)
                    )
                    total, seen, reds, greens, blues = state[j]
                    total = total + lax.log2(1.0 + jnp.exp2(dense))
                    now = jnp.exp2(signed_step * total)
                    weight = now - seen
                    after.append((
                        total,
                        now,
                        reds + weight * jnp.tanh(red),
                        greens + weight * jnp.tanh(green),
                        blues + weight * jnp.tanh(blue),
                    ))
                return tuple(after)

            zero = jnp.zeros((8, SPAN), jnp.float32)
            first = tuple((zero, zero + 1.0, zero, zero, zero) for j in range(GROUPS))
            last = lax.fori_loop(0, BLOCK, depth, first, unroll=True)
            for j in range(GROUPS):
                total, seen, reds, greens, blues = last[j]
                passed = jnp.exp2(total * -step_size)
                factor = jnp.where(down, 0.5 * passed, -0.5)
                spread = seen - 1.0
                planes = [factor * (spread + color) for color in (reds, greens, blues)]
                planes.append(1.0 - passed)
                for c in range(4):
                    for i in range(SPAN // LANES):
                        rows = pl.ds(j * (SPAN // LANES) + i, 8, stride=TILES)
                        stage_ref[half, c, rows, :] = planes[c][:, i * LANES:(i + 1) * LANES]
        for r in range(relative):
            slot = slot_ref[r]
            rows = pl.ds(pl.multiple_of(lax.rem(slot, 8) * TILES, TILES), TILES)
            for c in range(4):
                outs[r][0, c] = encode(stage_ref[slot // 8, c, rows, :])


def pinned(array):
    return pltpu.with_memory_space_constraint(array, pltpu.HBM)


def march(counts, order, flip, me, centers, amps, cells, step_size):
    tile_count = counts.shape[0]
    slots = cells.shape[0]
    capacity = slots // tile_count
    scalar = pl.BlockSpec(memory_space=pltpu.SMEM)
    whole = lambda shape: pl.BlockSpec(shape, lambda m: (0,) * len(shape))
    block = pl.BlockSpec((1, 4, TILES, LANES), lambda m: (m, 0, 0, 0))
    return pl.pallas_call(
        functools.partial(march_kernel, step_size, tile_count, tile_count),
        grid=(capacity,),
        in_specs=[scalar] * 4 + [
            whole((1, KNOTS)),
            whole((4, KNOTS)),
            pl.BlockSpec((tile_count, cells.shape[1]), lambda m: (m, 0)),
        ],
        out_specs=[block] * tile_count,
        out_shape=[jax.ShapeDtypeStruct((capacity, 4, TILES, LANES), jnp.int16)] * tile_count,
        scratch_shapes=[
            pltpu.VMEM((KNOTS, 8, LANES), jnp.float32),
            pltpu.VMEM((8 * STACK, 2 * KNOTS * STACK), jnp.bfloat16),
            pltpu.VMEM((tile_count // 8, 4, 8 * TILES, LANES), jnp.float32),
            pltpu.SMEM((tile_count,), jnp.int32),
        ],
        compiler_params=pltpu.CompilerParams(vmem_limit_bytes=GRANT),
        name="march",
    )(*(pinned(x) for x in (counts, order, flip, me, centers.reshape(1, KNOTS), amps, cells)))


def split_rows(image, kept_ref, given_ref, low, row_share):
    for n in range(kept_ref.shape[1] // row_share):
        mine = pl.multiple_of((2 * n + low) * row_share, row_share)
        theirs = pl.multiple_of((2 * n + 1 - low) * row_share, row_share)
        for c in range(4):
            kept_ref[c, n * row_share:(n + 1) * row_share] = image[c, pl.ds(mine, row_share)]
            given_ref[c, n * row_share:(n + 1) * row_share] = encode(image[c, pl.ds(theirs, row_share)])


def place_images(counts_ref, order_ref, me, brick_ref, arrived, tile_count):
    position = position_of(order_ref, me, tile_count)
    starts = [jnp.int32(0)]
    for i in range(tile_count):
        starts.append(starts[-1] + counts_ref[i])
    for r, images_ref in arrived:
        owner = lax.rem(me - r + tile_count, tile_count)
        start = jnp.int32(0)
        for i in range(tile_count):
            start = jnp.where(owner == i, starts[i], start)
        offset = lax.rem(position - start + tile_count * 64, tile_count)
        level = (start + offset - position) // tile_count
        held = (counts_ref[owner] - offset + tile_count - 1) // tile_count

        def place(m, carry, images_ref=images_ref, level=level):
            brick_ref[level + m] = decode(images_ref[m])
            return carry

        lax.fori_loop(0, held, place, 0)


def place_kernel(tile_count, *refs):
    counts_ref, order_ref, me_ref = refs[:3]
    arrived = [(r, ref) for r, ref in enumerate(refs[3:-1])]
    place_images(counts_ref, order_ref, me_ref[0], refs[-1], arrived, tile_count)


def place_early(counts, order, me, arrived):
    tile_count = counts.shape[0]
    scalar = pl.BlockSpec(memory_space=pltpu.SMEM)
    vmem = pl.BlockSpec(memory_space=pltpu.VMEM)
    brick = (DB * BY * BX, 4, TILES, LANES)
    return pl.pallas_call(
        functools.partial(place_kernel, tile_count),
        in_specs=[scalar] * 3 + [vmem] * len(arrived),
        out_specs=vmem,
        out_shape=jax.ShapeDtypeStruct(brick, jnp.float32),
        compiler_params=pltpu.CompilerParams(vmem_limit_bytes=GRANT),
        cost_estimate=pl.CostEstimate(flops=1 << 20, bytes_accessed=1 << 20, transcendentals=0),
        name="place",
    )(counts, order, me, *arrived)


def gather_kernel(tile_count, row_share, last_bit, *refs):
    counts_ref, order_ref, flip_ref, me_ref, layer_ref, early_ref = refs[:6]
    kept_ref, given_ref, front_ref, brick_ref, image_ref = refs[-5:]
    late = refs[6:-5]
    me = me_ref[0]
    brick_ref[...] = early_ref[...]
    arrived = [(tile_count - len(late) + n, ref) for n, ref in enumerate(late)]
    place_images(counts_ref, order_ref, me, brick_ref, arrived, tile_count)
    flip = flip_ref[me] == 1
    lane = lax.broadcasted_iota(jnp.int32, (TILES, LANES), 1) // BLOCK
    per_row = LANES // BLOCK
    for by in range(BY):
        images = []
        for bx in range(BX):
            layers = [(bz * BY + by) * BX + bx for bz in range(DB)]
            parts = None
            for n in range(DB):
                index = jnp.where(flip, layers[n], layers[DB - 1 - n])
                new = [brick_ref[index, c] for c in range(4)]
                if parts is None:
                    parts = new
                else:
                    uncovered = 1.0 - new[3]
                    parts = [new[c] + uncovered * parts[c] for c in range(4)]
            images.append(parts)
        for c in range(4):
            for s in range(per_row):
                line = None
                for bx in range(BX):
                    turn = (bx - s) * BLOCK % LANES
                    moved = images[bx][c]
                    if turn:
                        moved = pltpu.roll(moved, turn, 1)
                    line = moved if line is None else jnp.where(lane == bx, moved, line)
                image_ref[c, pl.ds(by * BLOCK + s, TILES, stride=per_row), :] = line
    split_rows(image_ref, kept_ref, given_ref, layer_ref[0] & 1, row_share)
    front = (layer_ref[0] >> last_bit & 1) == flip_ref[me]
    front_ref[...] = jnp.broadcast_to(jnp.where(front, 1.0, 0.0), (8, LANES))


def gather(counts, order, flip, me, layer, early, late, row_share, last_bit):
    tile_count = counts.shape[0]
    scalar = pl.BlockSpec(memory_space=pltpu.SMEM)
    vmem = pl.BlockSpec(memory_space=pltpu.VMEM)
    rows, width = BY * BLOCK, BX * BLOCK
    half = (4, rows // 2, width)
    return pl.pallas_call(
        functools.partial(gather_kernel, tile_count, row_share, last_bit),
        in_specs=[scalar] * 5 + [vmem] * (1 + len(late)),
        out_specs=[vmem] * 3,
        out_shape=[
            jax.ShapeDtypeStruct(half, jnp.float32),
            jax.ShapeDtypeStruct(half, jnp.int16),
            jax.ShapeDtypeStruct((8, LANES), jnp.float32),
        ],
        scratch_shapes=[
            pltpu.VMEM(early.shape, jnp.float32),
            pltpu.VMEM((4, rows, width), jnp.float32),
        ],
        compiler_params=pltpu.CompilerParams(vmem_limit_bytes=GRANT),
        name="gather",
    )(counts, order, flip, me, layer, early, *late)


def blend_kernel(bit, row_share, *refs):
    flip_ref, me_ref, layer_ref, kept_ref, other_ref, kept_out, given_out, image_ref = refs
    front = (layer_ref[0] >> bit & 1) == flip_ref[me_ref[0]]
    kept_open = 1.0 - kept_ref[3]
    other_open = 1.0 - decode(other_ref[3])
    kept_part = jnp.where(front, 1.0, other_open)
    other_part = jnp.where(front, kept_open, 1.0)
    for c in range(4):
        image_ref[c] = kept_part * kept_ref[c] + other_part * decode(other_ref[c])
    split_rows(image_ref, kept_out, given_out, layer_ref[0] >> (bit + 1) & 1, row_share)


def blend(flip, me, layer, kept, other, bit, row_share):
    scalar = pl.BlockSpec(memory_space=pltpu.SMEM)
    vmem = pl.BlockSpec(memory_space=pltpu.VMEM)
    half = (4, kept.shape[1] // 2, kept.shape[2])
    return pl.pallas_call(
        functools.partial(blend_kernel, bit, row_share),
        in_specs=[scalar] * 3 + [vmem] * 2,
        out_specs=[vmem] * 2,
        out_shape=[
            jax.ShapeDtypeStruct(half, jnp.float32),
            jax.ShapeDtypeStruct(half, jnp.int16),
        ],
        scratch_shapes=[pltpu.VMEM(kept.shape, jnp.float32)],
        compiler_params=pltpu.CompilerParams(vmem_limit_bytes=GRANT),
        name="blend",
    )(flip, me, layer, kept, other)


def last_blend(front, kept, coded):
    other = decode(coded)
    front = front[:1][None] > 0.5
    kept_part = jnp.where(front, 1.0, 1.0 - other[3:])
    other_part = jnp.where(front, 1.0 - kept[3:], 1.0)
    return kept_part * kept + other_part * other


def swapped(block, axis, bit):
    count = lax.axis_size(axis)
    return lax.ppermute(block, axis, [(i, i ^ 1 << bit) for i in range(count)])


def body(owned_blocks, slot_counts, brick_order, view_flip, tf_centers, tf_amps):
    tile_count = lax.axis_size("tile")
    depth_count = lax.axis_size("depth")
    step_size = 1.5 / (depth_count * DB * BLOCK)
    me = lax.axis_index("tile").astype(jnp.int32).reshape(1)
    layer = lax.axis_index("depth").astype(jnp.int32).reshape(1)
    counts, order = slot_counts[0], brick_order[0]
    inputs = (counts, order, view_flip, me, tf_centers, tf_amps, owned_blocks[0])
    sent = march(*inputs, step_size)
    arrived = [sent[0]]
    for r in range(1, tile_count):
        route = [(i, (i + r) % tile_count) for i in range(tile_count)]
        arrived.append(lax.ppermute(sent[r], "tile", route))
    early = place_early(counts, order, me, arrived[:tile_count // 2])
    row_share = BY * BLOCK // depth_count
    levels = depth_count.bit_length() - 1
    kept, given, front = gather(
        counts, order, view_flip, me, layer, early, arrived[tile_count // 2:], row_share, levels - 1
    )
    for bit in range(levels - 1):
        other = swapped(given, "depth", bit)
        kept, given = blend(view_flip, me, layer, kept, other, bit, row_share)
    return last_blend(front, kept, swapped(given, "depth", levels - 1))


def solution(mesh):
    in_specs = (P("depth", "tile", None), P("depth", None), P("depth", None), P(), P(), P())
    out_specs = P(None, "depth", "tile")
    return jax.shard_map(body, mesh=mesh, in_specs=in_specs, out_specs=out_specs, check_vma=False)
```

```python
import functools
import math

import jax
import jax.numpy as jnp
from jax import lax
from jax.experimental import pallas as pl
from jax.experimental.pallas import tpu as pltpu
from jax.sharding import PartitionSpec as P

BLOCK = 32
BX = 4
BY = 4
DB = 2
KNOTS = 8
PIXELS = BLOCK * BLOCK
LANES = 128
TILES = PIXELS // LANES
BUMP_SCALE = 4.0
LOG2E = math.log2(math.e)
ROOT = math.sqrt(BUMP_SCALE * LOG2E)
CODE_TOP = 65535.0
CODE_MID = 32768.0
GRANT = 12 << 20
SPAN = 512
GROUPS = PIXELS // SPAN
STACK = 8 * GROUPS
PACK = 16 // 8


def exclusive_start(counts_ref, index, tile_count):
    start = jnp.int32(0)
    for i in range(tile_count):
        start = start + jnp.where(i < index, counts_ref[i], 0)
    return start


def position_of(order_ref, tile, tile_count):
    position = jnp.int32(0)
    for i in range(tile_count):
        position = position + jnp.where(order_ref[i] == tile, i, 0)
    return position


def encode(image):
    root = jnp.exp2(jnp.log(jnp.maximum(image, 0.0)) * (0.25 * LOG2E))
    code = jnp.round(jnp.minimum(root, 1.0) * CODE_TOP - CODE_MID)
    return code.astype(jnp.int32).astype(jnp.int16)


def decode(code):
    root = (code.astype(jnp.int32).astype(jnp.float32) + CODE_MID) * (1.0 / CODE_TOP)
    square = root * root
    return square * square


def march_kernel(step_size, tile_count, relative, *refs):
    counts_ref, order_ref, flip_ref, me_ref, center_ref, amp_ref, cells_ref = refs[:7]
    outs = refs[7:7 + relative]
    coef_ref, mix_ref, stage_ref, slot_ref = refs[7 + relative:]
    step = pl.program_id(0)
    me = me_ref[0]
    start = exclusive_start(counts_ref, me, tile_count)
    live = counts_ref[me]

    @pl.when(step == 0)
    def _():
        for r in range(relative):
            tile = lax.rem(me + r, tile_count)
            slot_ref[r] = lax.rem(
                position_of(order_ref, tile, tile_count) - start + tile_count * 64, tile_count
            )
        w = center_ref[...] * ROOT
        folded = amp_ref[...] * jnp.exp2(-w * w)
        channel = lax.broadcasted_iota(jnp.int32, (4, 1), 0)
        folded = folded * jnp.where(channel == 3, LOG2E, 0.5)
        for k in range(KNOTS):
            coef_ref[k] = jnp.broadcast_to(2.0 * w[:, k:k + 1], (8, LANES))
        knot = lax.broadcasted_iota(jnp.int32, (4, KNOTS * STACK), 1) // STACK
        spread = jnp.zeros((4, KNOTS * STACK), jnp.float32)
        for k in range(KNOTS):
            spread = jnp.where(knot == k, folded[:, k:k + 1], spread)
        coarse = spread.astype(jnp.bfloat16)
        fine = (spread - coarse.astype(jnp.float32)).astype(jnp.bfloat16)
        own = lax.broadcasted_iota(jnp.int32, (STACK, KNOTS * STACK), 0) == lax.rem(
            lax.broadcasted_iota(jnp.int32, (STACK, KNOTS * STACK), 1), STACK
        )
        width = KNOTS * STACK
        for part, amps in enumerate((coarse, fine)):
            amps = amps.astype(jnp.float32)
            for c in range(4):
                first = (part * 4 + c) * STACK
                line = jnp.where(own, amps[c:c + 1], 0.0).astype(jnp.bfloat16)
                mix_ref[first:first + STACK, :width] = line
                mix_ref[first:first + STACK, width:] = line

    @pl.when(step * tile_count < live)
    def _():
        row = lax.broadcasted_iota(jnp.int32, (8, SPAN), 0)
        for half in range(tile_count // 8):
            flip = jnp.zeros((8, SPAN), jnp.int32)
            for s in range(8):
                tile = order_ref[lax.rem(start + half * 8 + s, tile_count)]
                flip = jnp.where(row == s, flip_ref[tile], flip)
            down = flip == 1
            signed_step = jnp.where(down, step_size, -step_size)

            def depth(z, state, half=half, signed_step=signed_step):
                values = []
                for j in range(GROUPS):
                    lane = pl.multiple_of(z * PIXELS + j * SPAN, LANES)
                    raw = cells_ref[half * 8:half * 8 + 8, pl.ds(lane, SPAN)]
                    values.append(raw.astype(jnp.float32) * ROOT)
                bumps = []
                for k in range(KNOTS):
                    center = jnp.concatenate([coef_ref[k]] * (SPAN // LANES), axis=1)
                    bumps += [jnp.exp2(v * (center - v)) for v in values]
                high, low = [], []
                for n in range(0, len(bumps), PACK):
                    bump = jnp.concatenate(bumps[n:n + PACK], axis=0)
                    coarse = bump.astype(jnp.bfloat16)
                    high.append(coarse)
                    low.append((bump - coarse.astype(jnp.float32)).astype(jnp.bfloat16))
                stacked = jnp.concatenate(high + low, axis=0)
                both = jnp.dot(mix_ref[...], stacked, preferred_element_type=jnp.float32)
                fields = both[:4 * STACK] + both[4 * STACK:]
                after = []
                for j in range(GROUPS):
                    red, green, blue, dense = (
                        fields[c * STACK + j * 8:c * STACK + j * 8 + 8] for c in range(4)
                    )
                    total, seen, reds, greens, blues = state[j]
                    total = total + lax.log2(1.0 + jnp.exp2(dense))
                    now = jnp.exp2(signed_step * total)
                    weight = now - seen
                    after.append((
                        total,
                        now,
                        reds + weight * jnp.tanh(red),
                        greens + weight * jnp.tanh(green),
                        blues + weight * jnp.tanh(blue),
                    ))
                return tuple(after)

            zero = jnp.zeros((8, SPAN), jnp.float32)
            first = tuple((zero, zero + 1.0, zero, zero, zero) for j in range(GROUPS))
            last = lax.fori_loop(0, BLOCK, depth, first, unroll=True)
            for j in range(GROUPS):
                total, seen, reds, greens, blues = last[j]
                passed = jnp.exp2(total * -step_size)
                factor = jnp.where(down, 0.5 * passed, -0.5)
                spread = seen - 1.0
                planes = [factor * (spread + color) for color in (reds, greens, blues)]
                planes.append(1.0 - passed)
                for c in range(4):
                    for i in range(SPAN // LANES):
                        rows = pl.ds(j * (SPAN // LANES) + i, 8, stride=TILES)
                        stage_ref[half, c, rows, :] = planes[c][:, i * LANES:(i + 1) * LANES]
        for r in range(relative):
            slot = slot_ref[r]
            rows = pl.ds(pl.multiple_of(lax.rem(slot, 8) * TILES, TILES), TILES)
            for c in range(4):
                outs[r][0, c] = encode(stage_ref[slot // 8, c, rows, :])


def pinned(array):
    return pltpu.with_memory_space_constraint(array, pltpu.HBM)


def march(counts, order, flip, me, centers, amps, cells, step_size):
    tile_count = counts.shape[0]
    slots = cells.shape[0]
    capacity = slots // tile_count
    scalar = pl.BlockSpec(memory_space=pltpu.SMEM)
    whole = lambda shape: pl.BlockSpec(shape, lambda m: (0,) * len(shape))
    block = pl.BlockSpec((1, 4, TILES, LANES), lambda m: (m, 0, 0, 0))
    return pl.pallas_call(
        functools.partial(march_kernel, step_size, tile_count, tile_count),
        grid=(capacity,),
        in_specs=[scalar] * 4 + [
            whole((1, KNOTS)),
            whole((4, KNOTS)),
            pl.BlockSpec((tile_count, cells.shape[1]), lambda m: (m, 0)),
        ],
        out_specs=[block] * tile_count,
        out_shape=[jax.ShapeDtypeStruct((capacity, 4, TILES, LANES), jnp.int16)] * tile_count,
        scratch_shapes=[
            pltpu.VMEM((KNOTS, 8, LANES), jnp.float32),
            pltpu.VMEM((8 * STACK, 2 * KNOTS * STACK), jnp.bfloat16),
            pltpu.VMEM((tile_count // 8, 4, 8 * TILES, LANES), jnp.float32),
            pltpu.SMEM((tile_count,), jnp.int32),
        ],
        compiler_params=pltpu.CompilerParams(vmem_limit_bytes=GRANT),
        name="march",
    )(*(pinned(x) for x in (counts, order, flip, me, centers.reshape(1, KNOTS), amps, cells)))


def split_rows(image, kept_ref, given_ref, low, row_share):
    for n in range(kept_ref.shape[1] // row_share):
        mine = pl.multiple_of((2 * n + low) * row_share, row_share)
        theirs = pl.multiple_of((2 * n + 1 - low) * row_share, row_share)
        for c in range(4):
            kept_ref[c, n * row_share:(n + 1) * row_share] = image[c, pl.ds(mine, row_share)]
            given_ref[c, n * row_share:(n + 1) * row_share] = encode(image[c, pl.ds(theirs, row_share)])


def place_images(counts_ref, order_ref, me, brick_ref, arrived, tile_count):
    position = position_of(order_ref, me, tile_count)
    starts = [jnp.int32(0)]
    for i in range(tile_count):
        starts.append(starts[-1] + counts_ref[i])
    for r, images_ref in arrived:
        owner = lax.rem(me - r + tile_count, tile_count)
        start = jnp.int32(0)
        for i in range(tile_count):
            start = jnp.where(owner == i, starts[i], start)
        offset = lax.rem(position - start + tile_count * 64, tile_count)
        level = (start + offset - position) // tile_count
        held = (counts_ref[owner] - offset + tile_count - 1) // tile_count

        def place(m, carry, images_ref=images_ref, level=level):
            brick_ref[level + m] = decode(images_ref[m])
            return carry

        lax.fori_loop(0, held, place, 0)


def place_kernel(tile_count, *refs):
    counts_ref, order_ref, me_ref = refs[:3]
    arrived = [(r, ref) for r, ref in enumerate(refs[3:-1])]
    place_images(counts_ref, order_ref, me_ref[0], refs[-1], arrived, tile_count)


def place_early(counts, order, me, arrived):
    tile_count = counts.shape[0]
    scalar = pl.BlockSpec(memory_space=pltpu.SMEM)
    vmem = pl.BlockSpec(memory_space=pltpu.VMEM)
    brick = (DB * BY * BX, 4, TILES, LANES)
    return pl.pallas_call(
        functools.partial(place_kernel, tile_count),
        in_specs=[scalar] * 3 + [vmem] * len(arrived),
        out_specs=vmem,
        out_shape=jax.ShapeDtypeStruct(brick, jnp.float32),
        compiler_params=pltpu.CompilerParams(vmem_limit_bytes=GRANT),
        cost_estimate=pl.CostEstimate(flops=1 << 20, bytes_accessed=1 << 20, transcendentals=0),
        name="place",
    )(counts, order, me, *arrived)


def gather_kernel(tile_count, row_share, last_bit, *refs):
    counts_ref, order_ref, flip_ref, me_ref, layer_ref, early_ref = refs[:6]
    kept_ref, given_ref, front_ref, brick_ref, image_ref = refs[-5:]
    late = refs[6:-5]
    me = me_ref[0]
    brick_ref[...] = early_ref[...]
    arrived = [(tile_count - len(late) + n, ref) for n, ref in enumerate(late)]
    place_images(counts_ref, order_ref, me, brick_ref, arrived, tile_count)
    flip = flip_ref[me] == 1
    lane = lax.broadcasted_iota(jnp.int32, (TILES, LANES), 1) // BLOCK
    per_row = LANES // BLOCK
    for by in range(BY):
        images = []
        for bx in range(BX):
            layers = [(bz * BY + by) * BX + bx for bz in range(DB)]
            parts = None
            for n in range(DB):
                index = jnp.where(flip, layers[n], layers[DB - 1 - n])
                new = [brick_ref[index, c] for c in range(4)]
                if parts is None:
                    parts = new
                else:
                    uncovered = 1.0 - new[3]
                    parts = [new[c] + uncovered * parts[c] for c in range(4)]
            images.append(parts)
        for c in range(4):
            for s in range(per_row):
                line = None
                for bx in range(BX):
                    turn = (bx - s) * BLOCK % LANES
                    moved = images[bx][c]
                    if turn:
                        moved = pltpu.roll(moved, turn, 1)
                    line = moved if line is None else jnp.where(lane == bx, moved, line)
                image_ref[c, pl.ds(by * BLOCK + s, TILES, stride=per_row), :] = line
    split_rows(image_ref, kept_ref, given_ref, layer_ref[0] & 1, row_share)
    front = (layer_ref[0] >> last_bit & 1) == flip_ref[me]
    front_ref[...] = jnp.broadcast_to(jnp.where(front, 1.0, 0.0), (8, LANES))


def gather(counts, order, flip, me, layer, early, late, row_share, last_bit):
    tile_count = counts.shape[0]
    scalar = pl.BlockSpec(memory_space=pltpu.SMEM)
    vmem = pl.BlockSpec(memory_space=pltpu.VMEM)
    rows, width = BY * BLOCK, BX * BLOCK
    half = (4, rows // 2, width)
    return pl.pallas_call(
        functools.partial(gather_kernel, tile_count, row_share, last_bit),
        in_specs=[scalar] * 5 + [vmem] * (1 + len(late)),
        out_specs=[vmem] * 3,
        out_shape=[
            jax.ShapeDtypeStruct(half, jnp.float32),
            jax.ShapeDtypeStruct(half, jnp.int16),
            jax.ShapeDtypeStruct((8, LANES), jnp.float32),
        ],
        scratch_shapes=[
            pltpu.VMEM(early.shape, jnp.float32),
            pltpu.VMEM((4, rows, width), jnp.float32),
        ],
        compiler_params=pltpu.CompilerParams(vmem_limit_bytes=GRANT),
        name="gather",
    )(counts, order, flip, me, layer, early, *late)


def blend_kernel(bit, row_share, *refs):
    flip_ref, me_ref, layer_ref, kept_ref, other_ref, kept_out, given_out, image_ref = refs
    front = (layer_ref[0] >> bit & 1) == flip_ref[me_ref[0]]
    kept_open = 1.0 - kept_ref[3]
    other_open = 1.0 - decode(other_ref[3])
    kept_part = jnp.where(front, 1.0, other_open)
    other_part = jnp.where(front, kept_open, 1.0)
    for c in range(4):
        image_ref[c] = kept_part * kept_ref[c] + other_part * decode(other_ref[c])
    split_rows(image_ref, kept_out, given_out, layer_ref[0] >> (bit + 1) & 1, row_share)


def blend(flip, me, layer, kept, other, bit, row_share):
    scalar = pl.BlockSpec(memory_space=pltpu.SMEM)
    vmem = pl.BlockSpec(memory_space=pltpu.VMEM)
    half = (4, kept.shape[1] // 2, kept.shape[2])
    return pl.pallas_call(
        functools.partial(blend_kernel, bit, row_share),
        in_specs=[scalar] * 3 + [vmem] * 2,
        out_specs=[vmem] * 2,
        out_shape=[
            jax.ShapeDtypeStruct(half, jnp.float32),
            jax.ShapeDtypeStruct(half, jnp.int16),
        ],
        scratch_shapes=[pltpu.VMEM(kept.shape, jnp.float32)],
        compiler_params=pltpu.CompilerParams(vmem_limit_bytes=GRANT),
        name="blend",
    )(flip, me, layer, kept, other)


def last_blend(front, kept, coded):
    other = decode(coded)
    front = front[:1][None] > 0.5
    kept_part = jnp.where(front, 1.0, 1.0 - other[3:])
    other_part = jnp.where(front, 1.0 - kept[3:], 1.0)
    return kept_part * kept + other_part * other


def swapped(block, axis, bit):
    count = lax.axis_size(axis)
    return lax.ppermute(block, axis, [(i, i ^ 1 << bit) for i in range(count)])


def body(owned_blocks, slot_counts, brick_order, view_flip, tf_centers, tf_amps):
    tile_count = lax.axis_size("tile")
    depth_count = lax.axis_size("depth")
    step_size = 1.5 / (depth_count * DB * BLOCK)
    me = lax.axis_index("tile").astype(jnp.int32).reshape(1)
    layer = lax.axis_index("depth").astype(jnp.int32).reshape(1)
    counts, order = slot_counts[0], brick_order[0]
    inputs = (counts, order, view_flip, me, tf_centers, tf_amps, owned_blocks[0])
    sent = march(*inputs, step_size)
    arrived = [sent[0]]
    for r in range(1, tile_count):
        route = [(i, (i + r) % tile_count) for i in range(tile_count)]
        arrived.append(lax.ppermute(sent[r], "tile", route))
    early = place_early(counts, order, me, arrived[:tile_count // 2])
    row_share = BY * BLOCK // depth_count
    levels = depth_count.bit_length() - 1
    kept, given, front = gather(
        counts, order, view_flip, me, layer, early, arrived[tile_count // 2:], row_share, levels - 1
    )
    for bit in range(levels - 1):
        other = swapped(given, "depth", bit)
        kept, given = blend(view_flip, me, layer, kept, other, bit, row_share)
    return last_blend(front, kept, swapped(given, "depth", levels - 1))


def solution(mesh):
    in_specs = (P("depth", "tile", None), P("depth", None), P("depth", None), P(), P(), P())
    out_specs = P(None, "depth", "tile")
    return jax.shard_map(body, mesh=mesh, in_specs=in_specs, out_specs=out_specs, check_vma=False)
```
